32 devices in a mesh: row: 8 (over y, x, core), col: 4 (over z).
Axes of the slice: x: 2, y: 2, z: 4, core: 2. Of those that a mesh axis runs over, the one named last changes fastest.
Arguments:
- design: bfloat16 [512, 90112], P(('row', 'col')), may hold values from -6 to 6
- arc_partials: float32 [32, 6, 16], P(('row', 'col')), may hold values from -6 to 6
- arc_id: int32 [32], P(('row', 'col')), may hold values from 0 to 7
- arc_weight: float32 [8], replicated, may hold values from 0.25 to 4
Outputs:
- normal_slab: float32 [90112, 2048], P('row', 'col')
The draws below stay inside these ranges and needn't reach their ends.
All inputs are finite; a program needn't handle non-finite values.
Results may differ from the reference program's by a relative error of at most 0.0003.
The reference program's roundings to bfloat16 on the way count: a program that leaves them out, or rounds other values in their place, can miss the bound.
Values may be sent and summed in bfloat16 or wider, within the bound.
A program may use at most 128 MiB of HBM per device.

```python
import math
import jax
import jax.numpy as jnp
from jax import lax

K = 90112
SLAB = 2048
E_DEV = 16
PARAMS = 6
ARCS = 8
SEGMENTS = 32
EPOCHS = 512


def with_ends(values, key, smallest, top_value):
    dims = values.shape
    place = [jax.random.randint(jax.random.fold_in(key, axis), (), 0, dims[axis]) for axis in range(len(dims))]
    values = values.at[tuple(place)].set(smallest)
    longest = dims.index(max(dims))
    place[longest] = (place[longest] + 1) % dims[longest]
    return values.at[tuple(place)].set(top_value)


def block_levels(key, extent, shards, low, top_value):
    level, own = 1.0, jax.random.fold_in(key, 6)
    for dim, shards_of in shards:
        steps = jnp.exp(jax.random.uniform(jax.random.fold_in(own, dim), (shards_of,), jnp.float32, low / len(shards), top_value / len(shards)))
        level = level * jnp.repeat(steps, extent[dim] // shards_of).reshape([-1 if axis == dim else 1 for axis in range(len(extent))])
    return level


def gaussian(key, shape, scale, bound, cuts=(), kind=jnp.bfloat16):
    drawn = jax.random.normal(key, shape, jnp.float32) * scale
    if len(cuts) > 0:
        drawn = block_levels(key, shape, cuts, -0.22, 0.18) * drawn
    return jnp.clip(drawn, min=-bound, max=bound).astype(kind)


def setup_inputs(seed: int = 0) -> dict:
    splits = jax.random.split(jax.random.key(seed), 5)
    design = gaussian(splits[0], (EPOCHS, K), 1.0, 6.0, ((0, 32),))
    arc_partials = gaussian(splits[1], (SEGMENTS, PARAMS, E_DEV), 1.0, 6.0, ((0, 32),), jnp.float32)
    arc_id = with_ends(jax.random.randint(splits[2], (SEGMENTS,), 0, ARCS), jax.random.fold_in(splits[2], 1), 0, ARCS - 1).astype(jnp.int32)
    arc_weight = jnp.clip(jnp.exp(jax.random.uniform(splits[3], (ARCS,), jnp.float32, math.log(0.25), math.log(4.0))), 0.25, 4.0)
    return dict(design=design, arc_partials=arc_partials, arc_id=arc_id, arc_weight=arc_weight)


ridge = 4.0


def solve_small(matrix, rhs):
    order = matrix.shape[-1]
    for pivot in range(order):
        scale = 1.0 / matrix[..., pivot, pivot]
        row_mat = matrix[..., pivot, :] * scale[..., None]
        row_rhs = rhs[..., pivot, :] * scale[..., None]
        factor = matrix[..., :, pivot]
        matrix = matrix - factor[..., :, None] * row_mat[..., None, :]
        rhs = rhs - factor[..., :, None] * row_rhs[..., None, :]
        matrix = matrix.at[..., pivot, :].set(row_mat)
        rhs = rhs.at[..., pivot, :].set(row_rhs)
    return rhs


def reference(design, arc_partials, arc_id, arc_weight):
    high = lax.Precision.HIGHEST
    segments = arc_partials.shape[0]
    slab_rows = design[:, :SLAB].astype(jnp.float32).reshape(segments, E_DEV, SLAB)
    coupling = jnp.einsum("npe,nes->nps", arc_partials, slab_rows, precision=high)
    gram = jnp.einsum("npe,nqe->npq", arc_partials, arc_partials, precision=high)
    arc_gram = jax.ops.segment_sum(gram, arc_id, ARCS)
    arc_coupling = jax.ops.segment_sum(coupling, arc_id, ARCS)
    own_gram = arc_gram[arc_id] + ridge * jnp.eye(PARAMS, dtype=jnp.float32)
    solved = solve_small(own_gram, arc_coupling[arc_id])
    reduced = slab_rows - jnp.einsum("npe,nps->nes", arc_partials, solved, precision=high)
    weights = arc_weight[arc_id]
    eliminated = (weights[:, None, None] * reduced).astype(jnp.bfloat16).reshape(EPOCHS, SLAB)
    product = jnp.dot(design.astype(jnp.float32).T, eliminated.astype(jnp.float32), precision=high, preferred_element_type=jnp.float32)
    return product * (1.0 / EPOCHS)
```

```python
import functools

import jax
import jax.numpy as jnp
from jax import lax
from jax.experimental import pallas as pl
from jax.experimental.pallas import tpu as pltpu
from jax.sharding import PartitionSpec as P

SLAB = 2048
LANES = 128
GROUP = 8
RIDGE = 4.0
SKEW = 1
SLAB_STEP = 3
SOLVE_STEP = 7
AHEAD = 3
SLOTS = 3

MESH = pl.DeviceIdType.MESH
HIGH = lax.Precision.HIGHEST


def chunk_width(rows):
    blocks = rows // LANES
    return LANES * max(k for k in range(1, 9) if blocks % k == 0)


def partner(r, p, count):
    out, bit = 0, 1
    while bit < count:
        out = out + bit * lax.rem(r // bit + p // bit, 2)
        bit *= 2
    return out


def dot(a, b, dims):
    return lax.dot_general(a, b, (dims, ((), ())), precision=HIGH, preferred_element_type=jnp.float32)


def eliminate(facts, values, order, arcs):
    wide = -(-arcs * GROUP // LANES) * LANES
    lane_in = lax.broadcasted_iota(jnp.int32, (LANES, wide), 0)
    lane_out = lax.broadcasted_iota(jnp.int32, (LANES, wide), 1)
    repeat = ((lane_in == lane_out % GROUP) & (lane_in < order)).astype(jnp.float32)
    number = (lane_in == order).astype(jnp.float32)
    partials = dot(facts, repeat, ((1,), (0,)))
    ids = dot(facts, number, ((1,), (0,)))
    arc = (lax.broadcasted_iota(jnp.int32, ids.shape, 1) // GROUP).astype(jnp.float32)
    spread = jnp.where(ids == arc, partials, 0.0)
    rhs = dot(spread, values, ((0,), (0,))).reshape(wide // GROUP, GROUP, -1)
    gram = dot(spread, facts, ((0,), (0,))).reshape(wide // GROUP, GROUP, LANES)
    at = lax.broadcasted_iota(jnp.int32, gram.shape, 1)
    gram = gram + jnp.where(at == lax.broadcasted_iota(jnp.int32, gram.shape, 2), RIDGE, 0.0)
    at_rhs = lax.broadcasted_iota(jnp.int32, rhs.shape, 1)
    for pivot in range(order):
        scale = 1.0 / gram[:, pivot : pivot + 1, pivot : pivot + 1]
        row_gram = gram[:, pivot : pivot + 1, :] * scale
        row_rhs = rhs[:, pivot : pivot + 1, :] * scale
        factor = gram[:, :, pivot : pivot + 1]
        gram = jnp.where(at == pivot, row_gram, gram - factor * row_gram)
        rhs = jnp.where(at_rhs == pivot, row_rhs, rhs - factor * row_rhs)
    fitted = dot(spread, rhs.reshape(wide, -1), ((1,), (0,)))
    return (facts[:, order + 1 : order + 2] * (values - fitted)).astype(jnp.bfloat16)


def gather_kernel(
    row_count, col_count, width,
    design, partials, ids, weights,
    held, out_elim,
    slab, facts, square,
    recv_z, send_down, send_up, recv_in, send_in, own_sem,
    slab_sem, facts_sem,
):
    r, c = lax.axis_index("row"), lax.axis_index("col")
    rows_dev, coefficients = design.shape
    rows = coefficients // row_count
    block = row_count * rows_dev
    columns = slab.shape[2]
    order, arcs = partials.shape[1], weights.shape[0]
    chunks = rows // width
    peers = [partner(r, p, row_count) for p in range(row_count)]

    square[...] = jnp.zeros_like(square)
    square[0:order, 0:rows_dev] = partials[0]
    square[order : order + 1, :] = jnp.full((1, LANES), ids[0].astype(jnp.float32))
    square[order + 1 : order + 2, :] = jnp.full((1, LANES), weights[ids[0]])
    facts[c, 0:rows_dev, :] = square[...].T[0:rows_dev, :]

    barrier = pltpu.get_barrier_semaphore()
    for p in range(1, row_count):
        pl.semaphore_signal(barrier, inc=1, device_id=(peers[p], c), device_id_type=MESH)
    for k in range(1, col_count):
        pl.semaphore_signal(barrier, inc=1, device_id=(r, lax.rem(c + k, col_count)), device_id_type=MESH)
    pl.semaphore_wait(barrier, row_count + col_count - 2)

    def remote(src, dst, send, recv, device):
        return pltpu.make_async_remote_copy(
            src_ref=src, dst_ref=dst, send_sem=send, recv_sem=recv, device_id=device, device_id_type=MESH
        )

    def arrived(ref, sem):
        pltpu.make_async_copy(ref, ref, sem).wait()

    def plane(z):
        return pl.multiple_of(z * block, block)

    def own_block(z):
        return held.at[pl.ds(plane(z), rows_dev), :]

    def chunk(z, j):
        return held.at[
            pl.ds(plane(z) + rows_dev, block - rows_dev), pl.ds(pl.multiple_of(j * width, width), width)
        ]

    mine = design.at[:, pl.ds(pl.multiple_of(r * rows, LANES), rows)]
    down, up = (r, lax.max(c - 1, 0)), (r, lax.min(c + 1, col_count - 1))

    @pl.when(c > 0)
    def _():
        remote(mine, own_block(c), send_down.at[c], recv_z.at[c, 0], down).start()

    @pl.when(c < col_count - 1)
    def _():
        remote(mine, own_block(c), send_up.at[c], recv_z.at[c, 0], up).start()

    def send_chunk(j):
        for p in range(1, row_count):
            start = pl.multiple_of(peers[p] * rows + j * width, LANES)
            remote(
                design.at[:, pl.ds(start, width)],
                held.at[
                    pl.ds(plane(c) + p * rows_dev, rows_dev), pl.ds(pl.multiple_of(j * width, width), width)
                ],
                send_in.at[0],
                recv_in.at[j],
                (peers[p], c),
            ).start()

    for j in range(min(AHEAD, chunks)):
        send_chunk(j)
    own_copy = pltpu.make_async_copy(mine, own_block(c), own_sem.at[0])
    own_copy.start()
    own_slab = pltpu.make_async_copy(
        design.at[:, pl.ds(pl.multiple_of(c * columns, LANES), columns)],
        slab.at[c, pl.ds(0, rows_dev), :],
        own_sem.at[1],
    )
    own_slab.start()
    for k in range(1, col_count):
        other = lax.rem(c + k, col_count)
        remote(
            design.at[:, pl.ds(pl.multiple_of(other * columns, LANES), columns)],
            slab.at[c, pl.ds(0, rows_dev), :],
            slab_sem.at[0],
            slab_sem.at[1],
            (r, other),
        ).start()
        remote(
            facts.at[c, pl.ds(0, rows_dev), :],
            facts.at[c, pl.ds(0, rows_dev), :],
            facts_sem.at[0],
            facts_sem.at[1],
            (r, other),
        ).start()

    def step(t, _):
        @pl.when((t + AHEAD - 1 < chunks) & (t >= 1))
        def _():
            send_chunk(t + AHEAD - 1)

        @pl.when((t >= 1) & (t <= chunks))
        def _():
            own = chunk(c, t - 1)
            arrived(own, recv_in.at[t - 1])

            @pl.when(c > 0)
            def _():
                remote(own, own, send_down.at[c], recv_z.at[c, t], down).start()

            @pl.when(c < col_count - 1)
            def _():
                remote(own, own, send_up.at[c], recv_z.at[c, t], up).start()

        for d in range(1, col_count):
            unit = t - d * SKEW
            for z, exists, onward, sems, target in (
                (c + d, c + d < col_count, c > 0, send_down, down),
                (c - d, c - d >= 0, c < col_count - 1, send_up, up),
            ):

                @pl.when((unit == 0) & exists)
                def _():
                    ref = own_block(z)
                    arrived(ref, recv_z.at[z, 0])

                    @pl.when(onward)
                    def _():
                        remote(ref, ref, sems.at[z], recv_z.at[z, 0], target).start()

                @pl.when((unit >= 1) & (unit <= chunks) & exists)
                def _():
                    ref = chunk(z, unit - 1)
                    arrived(ref, recv_z.at[z, unit])

                    @pl.when(onward)
                    def _():
                        remote(ref, ref, sems.at[z], recv_z.at[z, unit], target).start()

        @pl.when(t == SLAB_STEP)
        def _():
            own_slab.wait()
            arrived(slab.at[pl.ds(0, col_count - 1), pl.ds(0, rows_dev), :], slab_sem.at[1])
            arrived(facts.at[pl.ds(0, col_count - 1), pl.ds(0, rows_dev), :], facts_sem.at[1])
            for p in range(1, row_count):
                for ref, sem in ((slab, slab_sem), (facts, facts_sem)):
                    remote(
                        ref.at[:, pl.ds(0, rows_dev), :],
                        ref.at[:, pl.ds(p * rows_dev, rows_dev), :],
                        sem.at[2],
                        sem.at[3],
                        (peers[p], c),
                    ).start()

        @pl.when(t == SOLVE_STEP)
        def _():
            arrived(slab.at[:, pl.ds(rows_dev, block - rows_dev), :], slab_sem.at[3])
            arrived(facts.at[:, pl.ds(rows_dev, block - rows_dev), :], facts_sem.at[3])
            out_elim[...] = eliminate(
                facts[...].reshape(col_count * block, LANES),
                slab[...].reshape(col_count * block, columns).astype(jnp.float32),
                order,
                arcs,
            )

        return 0

    lax.fori_loop(0, chunks + 1 + (col_count - 1) * SKEW, step, 0)

    own_copy.wait()
    sent = design.at[:, pl.ds(0, (row_count - 1) * rows)]
    arrived(sent, send_in.at[0])
    for ref, sem in ((slab, slab_sem), (facts, facts_sem)):
        arrived(ref.at[pl.ds(0, col_count - 1), pl.ds(0, rows_dev), :], sem.at[0])
        arrived(ref.at[:, pl.ds(rows_dev, block - rows_dev), :], sem.at[2])
    for z in range(col_count):
        whole = held.at[pl.ds(z * block, block), :]

        @pl.when((c > 0) & (z >= c))
        def _():
            arrived(whole, send_down.at[z])

        @pl.when((c < col_count - 1) & (z <= c))
        def _():
            arrived(whole, send_up.at[z])


def gather(design, arc_partials, arc_id, arc_weight, row_count, col_count):
    rows_dev, coefficients = design.shape
    rows = coefficients // row_count
    epochs = rows_dev * row_count * col_count
    columns = SLAB // col_count
    block = rows_dev * row_count
    width = chunk_width(rows)
    chunks = rows // width
    dma = pltpu.SemaphoreType.DMA
    return pl.pallas_call(
        functools.partial(gather_kernel, row_count, col_count, width),
        out_shape=(
            pltpu.VMEM((epochs, rows), jnp.bfloat16),
            pltpu.VMEM((epochs, columns), jnp.bfloat16),
        ),
        in_specs=[
            pl.BlockSpec(memory_space=pl.ANY),
            pl.BlockSpec(memory_space=pltpu.VMEM),
            pl.BlockSpec(memory_space=pltpu.SMEM),
            pl.BlockSpec(memory_space=pltpu.SMEM),
        ],
        out_specs=(pl.BlockSpec(memory_space=pltpu.VMEM), pl.BlockSpec(memory_space=pltpu.VMEM)),
        scratch_shapes=[
            pltpu.VMEM((col_count, block, columns), jnp.bfloat16),
            pltpu.VMEM((col_count, block, LANES), jnp.float32),
            pltpu.VMEM((LANES, LANES), jnp.float32),
            dma((col_count, chunks + 1)),
            dma((col_count,)),
            dma((col_count,)),
            dma((chunks,)),
            dma((1,)),
            dma((2,)),
            dma((4,)),
            dma((4,)),
        ],
        compiler_params=pltpu.CompilerParams(
            collective_id=0, has_side_effects=True, vmem_limit_bytes=24 << 20
        ),
        name="gather",
    )(design, arc_partials, arc_id, arc_weight)


def product_kernel(scale, held, elim, out, tiles, sems):
    tile = tiles.shape[1]
    count = out.shape[0] // tile

    def copy(i):
        slot = lax.rem(i, SLOTS)
        return pltpu.make_async_copy(
            tiles.at[slot], out.at[pl.ds(pl.multiple_of(i * tile, tile), tile), :], sems.at[slot]
        )

    def step(i, _):
        @pl.when(i >= SLOTS)
        def _():
            copy(i - SLOTS).wait()

        tiles[lax.rem(i, SLOTS)] = scale * lax.dot_general(
            held[:, pl.ds(pl.multiple_of(i * tile, tile), tile)],
            elim[...],
            (((0,), (0,)), ((), ())),
            preferred_element_type=jnp.float32,
        )
        copy(i).start()
        return 0

    lax.fori_loop(0, count, step, 0)
    for i in range(max(0, count - SLOTS), count):
        copy(i).wait()


def product(held, elim):
    epochs, rows = held.shape
    columns = elim.shape[1]
    tile = chunk_width(rows)
    return pl.pallas_call(
        functools.partial(product_kernel, 1.0 / epochs),
        out_shape=jax.ShapeDtypeStruct((rows, columns), jnp.float32),
        in_specs=[pl.BlockSpec(memory_space=pltpu.VMEM), pl.BlockSpec(memory_space=pltpu.VMEM)],
        out_specs=pl.BlockSpec(memory_space=pl.ANY),
        scratch_shapes=[
            pltpu.VMEM((SLOTS, tile, columns), jnp.float32),
            pltpu.SemaphoreType.DMA((SLOTS,)),
        ],
        compiler_params=pltpu.CompilerParams(vmem_limit_bytes=24 << 20),
        cost_estimate=pl.CostEstimate(
            flops=2 * epochs * rows * columns, bytes_accessed=4 * rows * columns, transcendentals=0
        ),
        name="product",
    )(held, elim)


def local(design, arc_partials, arc_id, arc_weight):
    held, elim = gather(
        design, arc_partials, arc_id, arc_weight, lax.axis_size("row"), lax.axis_size("col")
    )
    return product(held, elim)


def solution(mesh):
    placed = (P(("row", "col"), None), P(("row", "col"), None, None), P(("row", "col")), P())
    return jax.shard_map(
        local, mesh=mesh, in_specs=placed, out_specs=P("row", "col"), check_vma=False
    )
```

```python
import functools

import jax
import jax.numpy as jnp
from jax import lax
from jax.experimental import pallas as pl
from jax.experimental.pallas import tpu as pltpu
from jax.sharding import PartitionSpec as P

SLAB = 2048
LANES = 128
GROUP = 8
RIDGE = 4.0
SKEW = 1
SLAB_STEP = 3
SOLVE_STEP = 7
AHEAD = 3
SLOTS = 3

MESH = pl.DeviceIdType.MESH
HIGH = lax.Precision.HIGHEST


def chunk_width(rows):
    blocks = rows // LANES
    return LANES * max(k for k in range(1, 9) if blocks % k == 0)


def partner(r, p, count):
    out, bit = 0, 1
    while bit < count:
        out = out + bit * lax.rem(r // bit + p // bit, 2)
        bit *= 2
    return out


def dot(a, b, dims):
    return lax.dot_general(a, b, (dims, ((), ())), precision=HIGH, preferred_element_type=jnp.float32)


def eliminate(facts, values, order, arcs):
    wide = -(-arcs * GROUP // LANES) * LANES
    lane_in = lax.broadcasted_iota(jnp.int32, (LANES, wide), 0)
    lane_out = lax.broadcasted_iota(jnp.int32, (LANES, wide), 1)
    repeat = ((lane_in == lane_out % GROUP) & (lane_in < order)).astype(jnp.float32)
    number = (lane_in == order).astype(jnp.float32)
    partials = dot(facts, repeat, ((1,), (0,)))
    ids = dot(facts, number, ((1,), (0,)))
    arc = (lax.broadcasted_iota(jnp.int32, ids.shape, 1) // GROUP).astype(jnp.float32)
    spread = jnp.where(ids == arc, partials, 0.0)
    rhs = dot(spread, values, ((0,), (0,))).reshape(wide // GROUP, GROUP, -1)
    gram = dot(spread, facts, ((0,), (0,))).reshape(wide // GROUP, GROUP, LANES)
    at = lax.broadcasted_iota(jnp.int32, gram.shape, 1)
    gram = gram + jnp.where(at == lax.broadcasted_iota(jnp.int32, gram.shape, 2), RIDGE, 0.0)
    at_rhs = lax.broadcasted_iota(jnp.int32, rhs.shape, 1)
    for pivot in range(order):
        scale = 1.0 / gram[:, pivot : pivot + 1, pivot : pivot + 1]
        row_gram = gram[:, pivot : pivot + 1, :] * scale
        row_rhs = rhs[:, pivot : pivot + 1, :] * scale
        factor = gram[:, :, pivot : pivot + 1]
        gram = jnp.where(at == pivot, row_gram, gram - factor * row_gram)
        rhs = jnp.where(at_rhs == pivot, row_rhs, rhs - factor * row_rhs)
    fitted = dot(spread, rhs.reshape(wide, -1), ((1,), (0,)))
    return (facts[:, order + 1 : order + 2] * (values - fitted)).astype(jnp.bfloat16)


def gather_kernel(
    row_count, col_count, width,
    design, partials_in, ids, weights_in,
    held, out_elim,
    slab, facts, square, partials, weights,
    recv_z, send_down, send_up, recv_in, send_in, own_sem,
    slab_sem, facts_sem,
):
    r, c = lax.axis_index("row"), lax.axis_index("col")
    rows_dev, coefficients = design.shape
    rows = coefficients // row_count
    block = row_count * rows_dev
    columns = slab.shape[2]
    order, arcs = partials.shape[0], weights.shape[0]
    chunks = rows // width
    peers = [partner(r, p, row_count) for p in range(row_count)]

    barrier = pltpu.get_barrier_semaphore()
    for p in range(1, row_count):
        pl.semaphore_signal(barrier, inc=1, device_id=(peers[p], c), device_id_type=MESH)
    for k in range(1, col_count):
        pl.semaphore_signal(barrier, inc=1, device_id=(r, lax.rem(c + k, col_count)), device_id_type=MESH)
    pl.semaphore_wait(barrier, row_count + col_count - 2)

    def remote(src, dst, send, recv, device):
        return pltpu.make_async_remote_copy(
            src_ref=src, dst_ref=dst, send_sem=send, recv_sem=recv, device_id=device, device_id_type=MESH
        )

    def arrived(ref, sem):
        pltpu.make_async_copy(ref, ref, sem).wait()

    def plane(z):
        return pl.multiple_of(z * block, block)

    def own_block(z):
        return held.at[pl.ds(plane(z), rows_dev), :]

    def chunk(z, j):
        return held.at[
            pl.ds(plane(z) + rows_dev, block - rows_dev), pl.ds(pl.multiple_of(j * width, width), width)
        ]

    mine = design.at[:, pl.ds(pl.multiple_of(r * rows, LANES), rows)]
    down, up = (r, lax.max(c - 1, 0)), (r, lax.min(c + 1, col_count - 1))

    @pl.when(c > 0)
    def _():
        remote(mine, own_block(c), send_down.at[c], recv_z.at[c, 0], down).start()

    @pl.when(c < col_count - 1)
    def _():
        remote(mine, own_block(c), send_up.at[c], recv_z.at[c, 0], up).start()

    def send_chunk(j):
        for p in range(1, row_count):
            start = pl.multiple_of(peers[p] * rows + j * width, LANES)
            remote(
                design.at[:, pl.ds(start, width)],
                held.at[
                    pl.ds(plane(c) + p * rows_dev, rows_dev), pl.ds(pl.multiple_of(j * width, width), width)
                ],
                send_in.at[0],
                recv_in.at[j],
                (peers[p], c),
            ).start()

    small = [
        pltpu.make_async_copy(src, dst, own_sem.at[2 + i])
        for i, (src, dst) in enumerate(((partials_in, partials), (weights_in, weights)))
    ]
    for copy in small:
        copy.start()
    for j in range(min(AHEAD, chunks)):
        send_chunk(j)
    own_copy = pltpu.make_async_copy(mine, own_block(c), own_sem.at[0])
    own_copy.start()
    own_slab = pltpu.make_async_copy(
        design.at[:, pl.ds(pl.multiple_of(c * columns, LANES), columns)],
        slab.at[c, pl.ds(0, rows_dev), :],
        own_sem.at[1],
    )
    own_slab.start()
    for copy in small:
        copy.wait()
    square[...] = jnp.zeros_like(square)
    for p in range(order):
        square[p : p + 1, 0:rows_dev] = partials[p]
    square[order : order + 1, :] = jnp.full((1, LANES), ids[0].astype(jnp.float32))
    square[order + 1 : order + 2, :] = jnp.full((1, LANES), weights[ids[0]])
    facts[c, 0:rows_dev, :] = square[...].T[0:rows_dev, :]
    for k in range(1, col_count):
        other = lax.rem(c + k, col_count)
        remote(
            design.at[:, pl.ds(pl.multiple_of(other * columns, LANES), columns)],
            slab.at[c, pl.ds(0, rows_dev), :],
            slab_sem.at[0],
            slab_sem.at[1],
            (r, other),
        ).start()
        remote(
            facts.at[c, pl.ds(0, rows_dev), :],
            facts.at[c, pl.ds(0, rows_dev), :],
            facts_sem.at[0],
            facts_sem.at[1],
            (r, other),
        ).start()

    def step(t, _):
        @pl.when((t + AHEAD - 1 < chunks) & (t >= 1))
        def _():
            send_chunk(t + AHEAD - 1)

        @pl.when((t >= 1) & (t <= chunks))
        def _():
            own = chunk(c, t - 1)
            arrived(own, recv_in.at[t - 1])

            @pl.when(c > 0)
            def _():
                remote(own, own, send_down.at[c], recv_z.at[c, t], down).start()

            @pl.when(c < col_count - 1)
            def _():
                remote(own, own, send_up.at[c], recv_z.at[c, t], up).start()

        for d in range(1, col_count):
            unit = t - d * SKEW
            for z, exists, onward, sems, target in (
                (c + d, c + d < col_count, c > 0, send_down, down),
                (c - d, c - d >= 0, c < col_count - 1, send_up, up),
            ):

                @pl.when((unit == 0) & exists)
                def _():
                    ref = own_block(z)
                    arrived(ref, recv_z.at[z, 0])

                    @pl.when(onward)
                    def _():
                        remote(ref, ref, sems.at[z], recv_z.at[z, 0], target).start()

                @pl.when((unit >= 1) & (unit <= chunks) & exists)
                def _():
                    ref = chunk(z, unit - 1)
                    arrived(ref, recv_z.at[z, unit])

                    @pl.when(onward)
                    def _():
                        remote(ref, ref, sems.at[z], recv_z.at[z, unit], target).start()

        @pl.when(t == SLAB_STEP)
        def _():
            own_slab.wait()
            arrived(slab.at[pl.ds(0, col_count - 1), pl.ds(0, rows_dev), :], slab_sem.at[1])
            arrived(facts.at[pl.ds(0, col_count - 1), pl.ds(0, rows_dev), :], facts_sem.at[1])
            for p in range(1, row_count):
                for ref, sem in ((slab, slab_sem), (facts, facts_sem)):
                    remote(
                        ref.at[:, pl.ds(0, rows_dev), :],
                        ref.at[:, pl.ds(p * rows_dev, rows_dev), :],
                        sem.at[2],
                        sem.at[3],
                        (peers[p], c),
                    ).start()

        @pl.when(t == SOLVE_STEP)
        def _():
            arrived(slab.at[:, pl.ds(rows_dev, block - rows_dev), :], slab_sem.at[3])
            arrived(facts.at[:, pl.ds(rows_dev, block - rows_dev), :], facts_sem.at[3])
            out_elim[...] = eliminate(
                facts[...].reshape(col_count * block, LANES),
                slab[...].reshape(col_count * block, columns).astype(jnp.float32),
                order,
                arcs,
            )

        return 0

    lax.fori_loop(0, chunks + 1 + (col_count - 1) * SKEW, step, 0)

    own_copy.wait()
    sent = design.at[:, pl.ds(0, (row_count - 1) * rows)]
    arrived(sent, send_in.at[0])
    for ref, sem in ((slab, slab_sem), (facts, facts_sem)):
        arrived(ref.at[pl.ds(0, col_count - 1), pl.ds(0, rows_dev), :], sem.at[0])
        arrived(ref.at[:, pl.ds(rows_dev, block - rows_dev), :], sem.at[2])
    for z in range(col_count):
        whole = held.at[pl.ds(z * block, block), :]

        @pl.when((c > 0) & (z >= c))
        def _():
            arrived(whole, send_down.at[z])

        @pl.when((c < col_count - 1) & (z <= c))
        def _():
            arrived(whole, send_up.at[z])


def in_hbm(array):
    return pltpu.with_memory_space_constraint(array, pltpu.HBM)


def gather(design, arc_partials, arc_id, arc_weight, row_count, col_count):
    rows_dev, coefficients = design.shape
    rows = coefficients // row_count
    epochs = rows_dev * row_count * col_count
    columns = SLAB // col_count
    block = rows_dev * row_count
    width = chunk_width(rows)
    chunks = rows // width
    dma = pltpu.SemaphoreType.DMA
    partials = arc_partials.transpose(1, 0, 2)
    return pl.pallas_call(
        functools.partial(gather_kernel, row_count, col_count, width),
        out_shape=(
            pltpu.VMEM((epochs, rows), jnp.bfloat16),
            pltpu.VMEM((epochs, columns), jnp.bfloat16),
        ),
        in_specs=[
            pl.BlockSpec(memory_space=pltpu.HBM),
            pl.BlockSpec(memory_space=pltpu.HBM),
            pl.BlockSpec(memory_space=pltpu.SMEM),
            pl.BlockSpec(memory_space=pltpu.HBM),
        ],
        out_specs=(pl.BlockSpec(memory_space=pltpu.VMEM), pl.BlockSpec(memory_space=pltpu.VMEM)),
        scratch_shapes=[
            pltpu.VMEM((col_count, block, columns), jnp.bfloat16),
            pltpu.VMEM((col_count, block, LANES), jnp.float32),
            pltpu.VMEM((LANES, LANES), jnp.float32),
            pltpu.VMEM(partials.shape, jnp.float32),
            pltpu.SMEM(arc_weight.shape, jnp.float32),
            dma((col_count, chunks + 1)),
            dma((col_count,)),
            dma((col_count,)),
            dma((chunks,)),
            dma((1,)),
            dma((4,)),
            dma((4,)),
            dma((4,)),
        ],
        compiler_params=pltpu.CompilerParams(
            collective_id=0, has_side_effects=True, vmem_limit_bytes=24 << 20
        ),
        name="gather",
    )(in_hbm(design), in_hbm(partials), arc_id, in_hbm(arc_weight))


def product_kernel(scale, held, elim, out, tiles, sems):
    tile = tiles.shape[1]
    count = out.shape[0] // tile

    def copy(i):
        slot = lax.rem(i, SLOTS)
        return pltpu.make_async_copy(
            tiles.at[slot], out.at[pl.ds(pl.multiple_of(i * tile, tile), tile), :], sems.at[slot]
        )

    def step(i, _):
        @pl.when(i >= SLOTS)
        def _():
            copy(i - SLOTS).wait()

        tiles[lax.rem(i, SLOTS)] = scale * lax.dot_general(
            held[:, pl.ds(pl.multiple_of(i * tile, tile), tile)],
            elim[...],
            (((0,), (0,)), ((), ())),
            preferred_element_type=jnp.float32,
        )
        copy(i).start()
        return 0

    lax.fori_loop(0, count, step, 0)
    for i in range(max(0, count - SLOTS), count):
        copy(i).wait()


def product(held, elim):
    epochs, rows = held.shape
    columns = elim.shape[1]
    tile = chunk_width(rows)
    return pl.pallas_call(
        functools.partial(product_kernel, 1.0 / epochs),
        out_shape=jax.ShapeDtypeStruct((rows, columns), jnp.float32),
        in_specs=[pl.BlockSpec(memory_space=pltpu.VMEM), pl.BlockSpec(memory_space=pltpu.VMEM)],
        out_specs=pl.BlockSpec(memory_space=pl.ANY),
        scratch_shapes=[
            pltpu.VMEM((SLOTS, tile, columns), jnp.float32),
            pltpu.SemaphoreType.DMA((SLOTS,)),
        ],
        compiler_params=pltpu.CompilerParams(vmem_limit_bytes=24 << 20),
        cost_estimate=pl.CostEstimate(
            flops=2 * epochs * rows * columns, bytes_accessed=4 * rows * columns, transcendentals=0
        ),
        name="product",
    )(held, elim)


def local(design, arc_partials, arc_id, arc_weight):
    held, elim = gather(
        design, arc_partials, arc_id, arc_weight, lax.axis_size("row"), lax.axis_size("col")
    )
    return product(held, elim)


def solution(mesh):
    placed = (P(("row", "col"), None), P(("row", "col"), None, None), P(("row", "col")), P())
    return jax.shard_map(
        local, mesh=mesh, in_specs=placed, out_specs=P("row", "col"), check_vma=False
    )
```

```python
import functools

import jax
import jax.numpy as jnp
from jax import lax
from jax.experimental import pallas as pl
from jax.experimental.pallas import tpu as pltpu
from jax.sharding import PartitionSpec as P

SLAB = 2048
LANES = 128
GROUP = 8
RIDGE = 4.0
SKEW = 1
AHEAD = 3
FACTS_STEP = 3
SOLVE_AFTER = 3

MESH = pl.DeviceIdType.MESH
HIGH = lax.Precision.HIGHEST


def chunk_width(rows):
    blocks = rows // LANES
    return LANES * max(k for k in range(1, 9) if blocks % k == 0)


def partner(r, p, count):
    out, bit = 0, 1
    while bit < count:
        out = out + bit * lax.rem(r // bit + p // bit, 2)
        bit *= 2
    return out


def dot(a, b, dims):
    return lax.dot_general(a, b, (dims, ((), ())), precision=HIGH, preferred_element_type=jnp.float32)


def eliminate(facts, values, order, arcs, rows_dev):
    wide = -(-arcs * GROUP // LANES) * LANES
    lane_in = lax.broadcasted_iota(jnp.int32, (LANES, wide), 0)
    lane_out = lax.broadcasted_iota(jnp.int32, (LANES, wide), 1)
    repeat = (lane_in // rows_dev == lane_out % GROUP).astype(jnp.float32)
    epoch = lax.broadcasted_iota(jnp.int32, facts.shape, 0)
    lane = lax.broadcasted_iota(jnp.int32, facts.shape, 1)
    own = (lane % rows_dev == epoch % rows_dev) & (lane < order * rows_dev)
    partials = dot(jnp.where(own, facts, 0.0), repeat, ((1,), (0,)))
    arc = (lax.broadcasted_iota(jnp.int32, partials.shape, 1) // GROUP).astype(jnp.float32)
    at_id = order * rows_dev
    spread = jnp.where(facts[:, at_id : at_id + 1] == arc, partials, 0.0)
    rhs = dot(spread, values, ((0,), (0,))).reshape(wide // GROUP, GROUP, -1)
    gram = dot(spread, partials[:, 0:LANES], ((0,), (0,))).reshape(wide // GROUP, GROUP, LANES)
    at = lax.broadcasted_iota(jnp.int32, gram.shape, 1)
    gram = gram + jnp.where(at == lax.broadcasted_iota(jnp.int32, gram.shape, 2), RIDGE, 0.0)
    at_rhs = lax.broadcasted_iota(jnp.int32, rhs.shape, 1)
    for pivot in range(order):
        scale = 1.0 / gram[:, pivot : pivot + 1, pivot : pivot + 1]
        row_gram = gram[:, pivot : pivot + 1, :] * scale
        row_rhs = rhs[:, pivot : pivot + 1, :] * scale
        factor = gram[:, :, pivot : pivot + 1]
        gram = jnp.where(at == pivot, row_gram, gram - factor * row_gram)
        rhs = jnp.where(at_rhs == pivot, row_rhs, rhs - factor * row_rhs)
    fitted = dot(spread, rhs.reshape(wide, -1), ((1,), (0,)))
    return (facts[:, at_id + 1 : at_id + 2] * (values - fitted)).astype(jnp.bfloat16)


def product_tile(held, elim, start, tile):
    epochs = elim.shape[0] * elim.shape[1]
    return (1.0 / epochs) * lax.dot_general(
        held[:, :, pl.ds(pl.multiple_of(start, tile), tile)].reshape(epochs, tile),
        elim[...].reshape(epochs, -1),
        (((0,), (0,)), ((), ())),
        preferred_element_type=jnp.float32,
    )


def gather_kernel(
    row_count, col_count, width,
    design, partials_in, ids, weights_in,
    held, elim, ready,
    slab, facts, spread_facts, partials, weights,
    recv_z, send_down, send_up, recv_in, send_in, own_sem,
    slab_sem, facts_sem,
):
    r, c = lax.axis_index("row"), lax.axis_index("col")
    rows_dev, coefficients = design.shape
    rows = coefficients // row_count
    block = row_count * rows_dev
    columns = slab.shape[2]
    order, arcs = partials.shape[0], weights.shape[0]
    chunks = rows // width
    slab_chunks = -(-columns * col_count // width)
    peers = [partner(r, p, row_count) for p in range(row_count)]

    barrier = pltpu.get_barrier_semaphore()
    for p in range(1, row_count):
        pl.semaphore_signal(barrier, inc=1, device_id=(peers[p], c), device_id_type=MESH)
    for k in range(1, col_count):
        pl.semaphore_signal(barrier, inc=1, device_id=(r, lax.rem(c + k, col_count)), device_id_type=MESH)
    pl.semaphore_wait(barrier, row_count + col_count - 2)

    def remote(src, dst, send, recv, device):
        return pltpu.make_async_remote_copy(
            src_ref=src, dst_ref=dst, send_sem=send, recv_sem=recv, device_id=device, device_id_type=MESH
        )

    def arrived(ref, sem):
        pltpu.make_async_copy(ref, ref, sem).wait()

    def own_block(z):
        return held.at[z, pl.ds(0, rows_dev), :]

    def part(j):
        return pl.ds(pl.multiple_of(j * width, width), width)

    def chunk(z, j):
        return held.at[z, pl.ds(rows_dev, block - rows_dev), part(j)]

    mine = design.at[:, pl.ds(pl.multiple_of(r * rows, LANES), rows)]
    down, up = (r, lax.max(c - 1, 0)), (r, lax.min(c + 1, col_count - 1))

    @pl.when(c > 0)
    def _():
        remote(mine, own_block(c), send_down.at[c], recv_z.at[c, 0], down).start()

    @pl.when(c < col_count - 1)
    def _():
        remote(mine, own_block(c), send_up.at[c], recv_z.at[c, 0], up).start()

    def send_chunk(j):
        for p in range(1, row_count):
            start = pl.multiple_of(peers[p] * rows + j * width, LANES)
            remote(
                design.at[:, pl.ds(start, width)],
                held.at[c, pl.ds(p * rows_dev, rows_dev), part(j)],
                send_in.at[0],
                recv_in.at[j],
                (peers[p], c),
            ).start()

    small = [
        pltpu.make_async_copy(src, dst, own_sem.at[1 + i])
        for i, (src, dst) in enumerate(((partials_in, partials), (weights_in, weights)))
    ]
    for copy in small:
        copy.start()
    for j in range(min(AHEAD, chunks)):
        send_chunk(j)
    own_copy = pltpu.make_async_copy(mine, own_block(c), own_sem.at[0])
    own_copy.start()

    for copy in small:
        copy.wait()
    lane = lax.broadcasted_iota(jnp.int32, (1, LANES), 1)
    row = jnp.where(lane == order * rows_dev, ids[0].astype(jnp.float32), 0.0)
    row = jnp.where(lane == order * rows_dev + 1, weights[ids[0]], row)
    shift_in = lax.broadcasted_iota(jnp.int32, (rows_dev, LANES), 0)
    shift_out = lax.broadcasted_iota(jnp.int32, (rows_dev, LANES), 1)
    for p in range(order):
        place = (shift_out == shift_in + p * rows_dev).astype(jnp.float32)
        row = row + dot(partials[p], place, ((1,), (0,)))
    facts[c, r] = row
    mine_facts = facts.at[c, r]
    for k in range(1, col_count):
        other = lax.rem(c + k, col_count)
        remote(mine_facts, mine_facts, facts_sem.at[0], facts_sem.at[1], (r, other)).start()
    others = facts.at[pl.ds(0, col_count - 1), 0]
    rest = facts.at[:, pl.ds(0, row_count - 1)]

    def step(t, _):
        @pl.when((t + AHEAD - 1 < chunks) & (t >= 1))
        def _():
            send_chunk(t + AHEAD - 1)

        @pl.when((t >= 1) & (t <= chunks))
        def _():
            own = chunk(c, t - 1)
            arrived(own, recv_in.at[t - 1])

            @pl.when(c > 0)
            def _():
                remote(own, own, send_down.at[c], recv_z.at[c, t], down).start()

            @pl.when(c < col_count - 1)
            def _():
                remote(own, own, send_up.at[c], recv_z.at[c, t], up).start()

        for d in range(1, col_count):
            unit = t - d * SKEW
            for z, exists, onward, sems, target in (
                (c + d, c + d < col_count, c > 0, send_down, down),
                (c - d, c - d >= 0, c < col_count - 1, send_up, up),
            ):

                @pl.when((unit == 0) & exists)
                def _():
                    ref = own_block(z)
                    arrived(ref, recv_z.at[z, 0])

                    @pl.when(onward)
                    def _():
                        remote(ref, ref, sems.at[z], recv_z.at[z, 0], target).start()

                @pl.when((unit >= 1) & (unit <= chunks) & exists)
                def _():
                    ref = chunk(z, unit - 1)
                    arrived(ref, recv_z.at[z, unit])

                    @pl.when(onward)
                    def _():
                        remote(ref, ref, sems.at[z], recv_z.at[z, unit], target).start()

        @pl.when(t == FACTS_STEP)
        def _():
            arrived(others, facts_sem.at[1])
            for p in range(1, row_count):
                ref = facts.at[:, r]
                remote(ref, ref, facts_sem.at[2], facts_sem.at[3], (peers[p], c)).start()

        @pl.when((t == slab_step) & (r == 0))
        def _():
            own_copy.wait()
            source = held.at[:, :, pl.ds(pl.multiple_of(c * columns, columns), columns)]
            for p in range(1, row_count):
                remote(source, slab, slab_sem.at[0], slab_sem.at[1], (p, c)).start()
            local_slab = pltpu.make_async_copy(source, slab, slab_sem.at[2])
            local_slab.start()
            local_slab.wait()

        @pl.when(t == solve_step)
        def _():
            @pl.when(r > 0)
            def _():
                own_copy.wait()
                arrived(slab, slab_sem.at[1])

            arrived(rest, facts_sem.at[3])
            for z in range(col_count):
                for k in range(row_count):
                    spread_facts[pl.ds((z * row_count + k) * rows_dev, rows_dev), :] = jnp.broadcast_to(
                        facts[z, k], (rows_dev, LANES)
                    )
            out = eliminate(
                spread_facts[...],
                slab[...].reshape(col_count * block, columns).astype(jnp.float32),
                order,
                arcs,
                rows_dev,
            ).reshape(col_count, block, columns)
            for k in range(row_count):
                at = pl.ds(pl.multiple_of(peers[k] * rows_dev, rows_dev), rows_dev)
                elim[:, at, :] = out[:, k * rows_dev : (k + 1) * rows_dev, :]

        here = lax.min(lax.max(t - (col_count - 1) * SKEW, 0), chunks - 1)
        before = lax.min(lax.max(t - 1 - (col_count - 1) * SKEW, 0), chunks - 1)

        @pl.when(t >= solve_step)
        def _():
            def form(j, _):
                ready[part(j), :] = product_tile(held, elim, j * width, width)
                return 0

            lax.fori_loop(lax.select(t == solve_step, 0, before), here, form, 0)

        return 0

    slab_step = slab_chunks + (col_count - 1) * SKEW
    solve_step = slab_step + SOLVE_AFTER
    lax.fori_loop(0, chunks + 1 + (col_count - 1) * SKEW, step, 0)

    sent = design.at[:, pl.ds(0, (row_count - 1) * rows)]
    arrived(sent, send_in.at[0])
    arrived(others, facts_sem.at[0])
    arrived(rest, facts_sem.at[2])

    @pl.when(r == 0)
    def _():
        share = held.at[:, :, pl.ds(0, (row_count - 1) * columns)]
        arrived(share, slab_sem.at[0])

    for z in range(col_count):
        whole = held.at[z]

        @pl.when((c > 0) & (z >= c))
        def _():
            arrived(whole, send_down.at[z])

        @pl.when((c < col_count - 1) & (z <= c))
        def _():
            arrived(whole, send_up.at[z])


def in_hbm(array):
    return pltpu.with_memory_space_constraint(array, pltpu.HBM)


def gather(design, arc_partials, arc_id, arc_weight, row_count, col_count):
    rows_dev, coefficients = design.shape
    rows = coefficients // row_count
    columns = SLAB // col_count
    block = rows_dev * row_count
    width = chunk_width(rows)
    chunks = rows // width
    dma = pltpu.SemaphoreType.DMA
    partials = arc_partials.transpose(1, 0, 2)
    in_vmem = pl.BlockSpec(memory_space=pltpu.VMEM)
    return pl.pallas_call(
        functools.partial(gather_kernel, row_count, col_count, width),
        out_shape=(
            pltpu.VMEM((col_count, block, rows), jnp.bfloat16),
            pltpu.VMEM((col_count, block, columns), jnp.bfloat16),
            pltpu.VMEM((rows - width, columns), jnp.float32),
        ),
        in_specs=[
            pl.BlockSpec(memory_space=pltpu.HBM),
            pl.BlockSpec(memory_space=pltpu.HBM),
            pl.BlockSpec(memory_space=pltpu.SMEM),
            pl.BlockSpec(memory_space=pltpu.HBM),
        ],
        out_specs=(in_vmem, in_vmem, in_vmem),
        scratch_shapes=[
            pltpu.VMEM((col_count, block, columns), jnp.bfloat16),
            pltpu.VMEM((col_count, row_count, 1, LANES), jnp.float32),
            pltpu.VMEM((col_count * block, LANES), jnp.float32),
            pltpu.VMEM(partials.shape, jnp.float32),
            pltpu.SMEM(arc_weight.shape, jnp.float32),
            dma((col_count, chunks + 1)),
            dma((col_count,)),
            dma((col_count,)),
            dma((chunks,)),
            dma((1,)),
            dma((3,)),
            dma((3,)),
            dma((4,)),
        ],
        compiler_params=pltpu.CompilerParams(
            collective_id=0, has_side_effects=True, vmem_limit_bytes=16 << 20
        ),
        name="gather",
    )(in_hbm(design), in_hbm(partials), arc_id, in_hbm(arc_weight))


def finish_kernel(held, elim, ready, out, tile, sems):
    size = tile.shape[0]
    count = out.shape[0] // size - 1

    def copy(i):
        at = pl.ds(i * size, size)
        return pltpu.make_async_copy(tile if i == count else ready.at[at, :], out.at[at, :], sems.at[i])

    for i in range(count):
        copy(i).start()
    tile[...] = product_tile(held, elim, count * size, size)
    copy(count).start()
    for i in range(count + 1):
        copy(i).wait()


def finish(held, elim, ready):
    col_count, block, rows = held.shape
    columns = elim.shape[2]
    width = chunk_width(rows)
    in_vmem = pl.BlockSpec(memory_space=pltpu.VMEM)
    return pl.pallas_call(
        finish_kernel,
        out_shape=jax.ShapeDtypeStruct((rows, columns), jnp.float32),
        in_specs=[in_vmem, in_vmem, in_vmem],
        out_specs=pl.BlockSpec(memory_space=pl.ANY),
        scratch_shapes=[
            pltpu.VMEM((width, columns), jnp.float32),
            pltpu.SemaphoreType.DMA((rows // width,)),
        ],
        compiler_params=pltpu.CompilerParams(vmem_limit_bytes=16 << 20),
        cost_estimate=pl.CostEstimate(
            flops=2 * col_count * block * width * columns,
            bytes_accessed=4 * rows * columns,
            transcendentals=0,
        ),
        name="finish",
    )(held, elim, ready)


def local(design, arc_partials, arc_id, arc_weight):
    return finish(
        *gather(design, arc_partials, arc_id, arc_weight, lax.axis_size("row"), lax.axis_size("col"))
    )


def solution(mesh):
    placed = (P(("row", "col"), None), P(("row", "col"), None, None), P(("row", "col")), P())
    return jax.shard_map(
        local, mesh=mesh, in_specs=placed, out_specs=P("row", "col"), check_vma=False
    )
```

```python
import functools

import jax
import jax.numpy as jnp
from jax import lax
from jax.experimental import pallas as pl
from jax.experimental.pallas import tpu as pltpu
from jax.sharding import PartitionSpec as P

SLAB = 2048
LANES = 128
GROUP = 8
RIDGE = 4.0
SKEW = 1
AHEAD = 3
FACTS_STEP = 3
SOLVE_AFTER = 3
LEFT = 2

MESH = pl.DeviceIdType.MESH
HIGH = lax.Precision.HIGHEST


def chunk_width(rows):
    blocks = rows // LANES
    return LANES * max(k for k in range(1, 9) if blocks % k == 0)


def partner(r, p, count):
    out, bit = 0, 1
    while bit < count:
        out = out + bit * lax.rem(r // bit + p // bit, 2)
        bit *= 2
    return out


def dot(a, b, dims):
    return lax.dot_general(a, b, (dims, ((), ())), precision=HIGH, preferred_element_type=jnp.float32)


def eliminate(facts, values, order, arcs, rows_dev):
    wide = -(-arcs * GROUP // LANES) * LANES
    lane_in = lax.broadcasted_iota(jnp.int32, (LANES, wide), 0)
    lane_out = lax.broadcasted_iota(jnp.int32, (LANES, wide), 1)
    repeat = (lane_in // rows_dev == lane_out % GROUP).astype(jnp.float32)
    epoch = lax.broadcasted_iota(jnp.int32, facts.shape, 0)
    lane = lax.broadcasted_iota(jnp.int32, facts.shape, 1)
    own = (lane % rows_dev == epoch % rows_dev) & (lane < order * rows_dev)
    partials = dot(jnp.where(own, facts, 0.0), repeat, ((1,), (0,)))
    arc = (lax.broadcasted_iota(jnp.int32, partials.shape, 1) // GROUP).astype(jnp.float32)
    at_id = order * rows_dev
    spread = jnp.where(facts[:, at_id : at_id + 1] == arc, partials, 0.0)
    rhs = dot(spread, values, ((0,), (0,))).reshape(wide // GROUP, GROUP, -1)
    gram = dot(spread, partials[:, 0:LANES], ((0,), (0,))).reshape(wide // GROUP, GROUP, LANES)
    at = lax.broadcasted_iota(jnp.int32, gram.shape, 1)
    gram = gram + jnp.where(at == lax.broadcasted_iota(jnp.int32, gram.shape, 2), RIDGE, 0.0)
    at_rhs = lax.broadcasted_iota(jnp.int32, rhs.shape, 1)
    for pivot in range(order):
        scale = 1.0 / gram[:, pivot : pivot + 1, pivot : pivot + 1]
        row_gram = gram[:, pivot : pivot + 1, :] * scale
        row_rhs = rhs[:, pivot : pivot + 1, :] * scale
        factor = gram[:, :, pivot : pivot + 1]
        gram = jnp.where(at == pivot, row_gram, gram - factor * row_gram)
        rhs = jnp.where(at_rhs == pivot, row_rhs, rhs - factor * row_rhs)
    fitted = dot(spread, rhs.reshape(wide, -1), ((1,), (0,)))
    return (facts[:, at_id + 1 : at_id + 2] * (values - fitted)).astype(jnp.bfloat16)


def product_tile(held, elim, start, tile):
    epochs = elim.shape[0] * elim.shape[1]
    return (1.0 / epochs) * lax.dot_general(
        held[:, :, pl.ds(pl.multiple_of(start, tile), tile)].reshape(epochs, tile),
        elim[...].reshape(epochs, -1),
        (((0,), (0,)), ((), ())),
        preferred_element_type=jnp.float32,
    )


def gather_kernel(
    row_count, col_count, width,
    design, partials_in, ids, weights_in,
    held, elim, ready, piece,
    slab, facts, spread_facts, partials, weights,
    recv_z, own_down, own_up, send_down, send_up, recv_in, send_in, own_sem,
    slab_sem, facts_sem,
):
    r, c = lax.axis_index("row"), lax.axis_index("col")
    rows_dev, coefficients = design.shape
    rows = coefficients // row_count
    block = row_count * rows_dev
    columns = slab.shape[2]
    order, arcs = partials.shape[0], weights.shape[0]
    chunks = rows // width
    slab_chunks = -(-columns * col_count // width)
    peers = [partner(r, p, row_count) for p in range(row_count)]

    barrier = pltpu.get_barrier_semaphore()
    for p in range(1, row_count):
        pl.semaphore_signal(barrier, inc=1, device_id=(peers[p], c), device_id_type=MESH)
    for k in range(1, col_count):
        pl.semaphore_signal(barrier, inc=1, device_id=(r, lax.rem(c + k, col_count)), device_id_type=MESH)
    pl.semaphore_wait(barrier, row_count + col_count - 2)

    def remote(src, dst, send, recv, device):
        return pltpu.make_async_remote_copy(
            src_ref=src, dst_ref=dst, send_sem=send, recv_sem=recv, device_id=device, device_id_type=MESH
        )

    def arrived(ref, sem):
        pltpu.make_async_copy(ref, ref, sem).wait()

    def own_block(z):
        return held.at[z, pl.ds(0, rows_dev), :]

    def part(j):
        return pl.ds(pl.multiple_of(j * width, width), width)

    def chunk(z, j):
        return held.at[z, pl.ds(rows_dev, block - rows_dev), part(j)]

    mine = design.at[:, pl.ds(pl.multiple_of(r * rows, LANES), rows)]
    down, up = (r, lax.max(c - 1, 0)), (r, lax.min(c + 1, col_count - 1))

    @pl.when(c > 0)
    def _():
        remote(mine, own_block(c), own_down.at[c], recv_z.at[c, 0], down).start()

    @pl.when(c < col_count - 1)
    def _():
        remote(mine, own_block(c), own_up.at[c], recv_z.at[c, 0], up).start()

    def send_chunk(j):
        for p in range(1, row_count):
            start = pl.multiple_of(peers[p] * rows + j * width, LANES)
            remote(
                design.at[:, pl.ds(start, width)],
                held.at[c, pl.ds(p * rows_dev, rows_dev), part(j)],
                send_in.at[0],
                recv_in.at[j],
                (peers[p], c),
            ).start()

    small = [
        pltpu.make_async_copy(src, dst, own_sem.at[1 + i])
        for i, (src, dst) in enumerate(((partials_in, partials), (weights_in, weights)))
    ]
    for copy in small:
        copy.start()
    for j in range(min(AHEAD, chunks)):
        send_chunk(j)
    own_copy = pltpu.make_async_copy(mine, own_block(c), own_sem.at[0])
    own_copy.start()

    for copy in small:
        copy.wait()
    lane = lax.broadcasted_iota(jnp.int32, (1, LANES), 1)
    row = jnp.where(lane == order * rows_dev, ids[0].astype(jnp.float32), 0.0)
    row = jnp.where(lane == order * rows_dev + 1, weights[ids[0]], row)
    shift_in = lax.broadcasted_iota(jnp.int32, (rows_dev, LANES), 0)
    shift_out = lax.broadcasted_iota(jnp.int32, (rows_dev, LANES), 1)
    for p in range(order):
        place = (shift_out == shift_in + p * rows_dev).astype(jnp.float32)
        row = row + dot(partials[p], place, ((1,), (0,)))
    facts[c, r] = row
    mine_facts = facts.at[c, r]
    for k in range(1, col_count):
        other = lax.rem(c + k, col_count)
        remote(mine_facts, mine_facts, facts_sem.at[0], facts_sem.at[1], (r, other)).start()
    others = facts.at[pl.ds(0, col_count - 1), 0]
    rest = facts.at[:, pl.ds(0, row_count - 1)]

    def step(t, _):
        @pl.when((t + AHEAD - 1 < chunks) & (t >= 1))
        def _():
            send_chunk(t + AHEAD - 1)

        @pl.when((t >= 1) & (t <= chunks))
        def _():
            own = chunk(c, t - 1)
            arrived(own, recv_in.at[t - 1])

            @pl.when(c > 0)
            def _():
                remote(own, own, send_down.at[c], recv_z.at[c, t], down).start()

            @pl.when(c < col_count - 1)
            def _():
                remote(own, own, send_up.at[c], recv_z.at[c, t], up).start()

        for d in range(1, col_count):
            unit = t - d * SKEW
            for z, exists, onward, own_sems, sems, target in (
                (c + d, c + d < col_count, c > 0, own_down, send_down, down),
                (c - d, c - d >= 0, c < col_count - 1, own_up, send_up, up),
            ):

                @pl.when((unit == 0) & exists)
                def _():
                    ref = own_block(z)
                    arrived(ref, recv_z.at[z, 0])

                    @pl.when(onward)
                    def _():
                        remote(ref, ref, own_sems.at[z], recv_z.at[z, 0], target).start()

                units = chunks if d < col_count - 1 else chunks - 1

                @pl.when((unit >= 1) & (unit <= units) & exists)
                def _():
                    ref = chunk(z, unit - 1)
                    arrived(ref, recv_z.at[z, unit])
                    sends = onward if d < col_count - 2 else onward & (unit < chunks)

                    @pl.when(sends)
                    def _():
                        remote(ref, ref, sems.at[z], recv_z.at[z, unit], target).start()

                    if d == col_count - 2:

                        @pl.when(onward & (unit == chunks))
                        def _():
                            pltpu.make_async_copy(ref, piece, own_sem.at[3]).start()

        @pl.when(t == FACTS_STEP)
        def _():
            arrived(others, facts_sem.at[1])
            for p in range(1, row_count):
                ref = facts.at[:, r]
                remote(ref, ref, facts_sem.at[2], facts_sem.at[3], (peers[p], c)).start()

        @pl.when((t == slab_step) & (r == 0))
        def _():
            own_copy.wait()
            source = held.at[:, :, pl.ds(pl.multiple_of(c * columns, columns), columns)]
            for p in range(1, row_count):
                remote(source, slab, slab_sem.at[0], slab_sem.at[1], (p, c)).start()
            local_slab = pltpu.make_async_copy(source, slab, slab_sem.at[2])
            local_slab.start()
            local_slab.wait()

        @pl.when(t == solve_step)
        def _():
            @pl.when(r > 0)
            def _():
                own_copy.wait()
                arrived(slab, slab_sem.at[1])

            arrived(rest, facts_sem.at[3])
            for z in range(col_count):
                for k in range(row_count):
                    spread_facts[pl.ds((z * row_count + k) * rows_dev, rows_dev), :] = jnp.broadcast_to(
                        facts[z, k], (rows_dev, LANES)
                    )
            out = eliminate(
                spread_facts[...],
                slab[...].reshape(col_count * block, columns).astype(jnp.float32),
                order,
                arcs,
                rows_dev,
            ).reshape(col_count, block, columns)
            for edge, far in ((0, col_count - 1), (col_count - 1, 0)):

                @pl.when(c == edge)
                def _():
                    held[far, rows_dev:block, rows - width : rows] = jnp.zeros(
                        (block - rows_dev, width), jnp.bfloat16
                    )

            for k in range(row_count):
                at = pl.ds(pl.multiple_of(peers[k] * rows_dev, rows_dev), rows_dev)
                elim[:, at, :] = out[:, k * rows_dev : (k + 1) * rows_dev, :]

        here = lax.min(lax.max(t - (col_count - 1) * SKEW, 0), chunks - LEFT)
        before = lax.min(lax.max(t - 1 - (col_count - 1) * SKEW, 0), chunks - LEFT)

        @pl.when(t >= solve_step)
        def _():
            def form(j, _):
                ready[part(j), :] = product_tile(held, elim, j * width, width)
                return 0

            lax.fori_loop(lax.select(t == solve_step, 0, before), here, form, 0)

        return 0

    slab_step = slab_chunks + (col_count - 1) * SKEW
    solve_step = slab_step + SOLVE_AFTER
    lax.fori_loop(0, chunks + 1 + (col_count - 1) * SKEW, step, 0)

    sent = design.at[:, pl.ds(0, (row_count - 1) * rows)]
    arrived(sent, send_in.at[0])
    arrived(others, facts_sem.at[0])
    arrived(rest, facts_sem.at[2])

    @pl.when(r == 0)
    def _():
        share = held.at[:, :, pl.ds(0, (row_count - 1) * columns)]
        arrived(share, slab_sem.at[0])

    for z in range(col_count):
        others_of = held.at[z, pl.ds(rows_dev, block - rows_dev), :]
        shorter = held.at[z, pl.ds(rows_dev, block - rows_dev), pl.ds(0, rows - width)]
        for sends, far, last_hop, own_sems, sems in (
            ((c > 0) & (z >= c), col_count - 1, c == 1, own_down, send_down),
            ((c < col_count - 1) & (z <= c), 0, c == col_count - 2, own_up, send_up),
        ):

            @pl.when(sends)
            def _():
                arrived(own_block(z), own_sems.at[z])

            if z == far:

                @pl.when(sends & last_hop)
                def _():
                    arrived(shorter, sems.at[z])
                    arrived(piece, own_sem.at[3])

                sends = sends & jnp.logical_not(last_hop)

            @pl.when(sends)
            def _():
                arrived(others_of, sems.at[z])


def in_hbm(array):
    return pltpu.with_memory_space_constraint(array, pltpu.HBM)


def gather(design, arc_partials, arc_id, arc_weight, row_count, col_count):
    rows_dev, coefficients = design.shape
    rows = coefficients // row_count
    columns = SLAB // col_count
    block = rows_dev * row_count
    width = chunk_width(rows)
    chunks = rows // width
    dma = pltpu.SemaphoreType.DMA
    partials = arc_partials.transpose(1, 0, 2)
    in_vmem = pl.BlockSpec(memory_space=pltpu.VMEM)
    return pl.pallas_call(
        functools.partial(gather_kernel, row_count, col_count, width),
        out_shape=(
            pltpu.VMEM((col_count, block, rows), jnp.bfloat16),
            pltpu.VMEM((col_count, block, columns), jnp.bfloat16),
            pltpu.VMEM((rows - LEFT * width, columns), jnp.float32),
            pltpu.VMEM((block - rows_dev, width), jnp.bfloat16),
        ),
        in_specs=[
            pl.BlockSpec(memory_space=pltpu.HBM),
            pl.BlockSpec(memory_space=pltpu.HBM),
            pl.BlockSpec(memory_space=pltpu.SMEM),
            pl.BlockSpec(memory_space=pltpu.HBM),
        ],
        out_specs=(in_vmem,) * 4,
        scratch_shapes=[
            pltpu.VMEM((col_count, block, columns), jnp.bfloat16),
            pltpu.VMEM((col_count, row_count, 1, LANES), jnp.float32),
            pltpu.VMEM((col_count * block, LANES), jnp.float32),
            pltpu.VMEM(partials.shape, jnp.float32),
            pltpu.SMEM(arc_weight.shape, jnp.float32),
            dma((col_count, chunks + 1)),
            dma((col_count,)),
            dma((col_count,)),
            dma((col_count,)),
            dma((col_count,)),
            dma((chunks,)),
            dma((1,)),
            dma((4,)),
            dma((3,)),
            dma((4,)),
        ],
        compiler_params=pltpu.CompilerParams(
            collective_id=0, has_side_effects=True, vmem_limit_bytes=16 << 20
        ),
        name="gather",
    )(in_hbm(design), in_hbm(partials), arc_id, in_hbm(arc_weight))


def finish_kernel(held, elim, ready, out, partial, tile, sems):
    size = partial.shape[0]
    count = ready.shape[0] // size

    def copy(i):
        at = pl.ds(i * size, size)
        source = ready.at[at, :] if i < count else tile.at[i - count]
        return pltpu.make_async_copy(source, out.at[at, :], sems.at[i])

    for i in range(count):
        copy(i).start()
    for i in range(count, count + LEFT - 1):
        tile[i - count] = product_tile(held, elim, i * size, size)
        copy(i).start()
    partial[...] = product_tile(held, elim, (count + LEFT - 1) * size, size)
    for i in range(count + LEFT - 1):
        copy(i).wait()


def finish(held, elim, ready):
    col_count, block, rows = held.shape
    columns = elim.shape[2]
    width = chunk_width(rows)
    in_vmem = pl.BlockSpec(memory_space=pltpu.VMEM)
    return pl.pallas_call(
        finish_kernel,
        out_shape=(
            jax.ShapeDtypeStruct((rows, columns), jnp.float32),
            pltpu.VMEM((width, columns), jnp.float32),
        ),
        in_specs=[in_vmem, in_vmem, in_vmem],
        out_specs=(pl.BlockSpec(memory_space=pl.ANY), in_vmem),
        scratch_shapes=[
            pltpu.VMEM((LEFT - 1, width, columns), jnp.float32),
            pltpu.SemaphoreType.DMA((rows // width - 1,)),
        ],
        compiler_params=pltpu.CompilerParams(vmem_limit_bytes=12 << 20),
        cost_estimate=pl.CostEstimate(
            flops=2 * LEFT * col_count * block * width * columns,
            bytes_accessed=4 * rows * columns,
            transcendentals=0,
        ),
        name="finish",
    )(held, elim, ready)


def last_kernel(scale, rows_dev, elim, partial, arrived, total, out, tile, sems):
    col_count, block, _ = elim.shape
    width = partial.shape[0]
    half = width // 2
    far = lax.select(lax.axis_index("col") == 0, col_count - 1, 0)
    copies = []
    for i in range(2):
        at = pl.ds(i * half, half)
        tile[at, :] = partial[at, :] + scale * lax.dot_general(
            arrived[:, at],
            elim[far, rows_dev:block, :],
            (((0,), (0,)), ((), ())),
            preferred_element_type=jnp.float32,
        )
        to = pl.ds(out.shape[0] - width + i * half, half)
        copies.append(pltpu.make_async_copy(tile.at[at, :], out.at[to, :], sems.at[i]))
        copies[i].start()
    for copy in copies:
        copy.wait()


def last(elim, partial, arrived, total, rows_dev):
    col_count, block, columns = elim.shape
    width = partial.shape[0]
    in_vmem = pl.BlockSpec(memory_space=pltpu.VMEM)
    in_place = pl.BlockSpec(memory_space=pl.ANY)
    return pl.pallas_call(
        functools.partial(last_kernel, 1.0 / (col_count * block), rows_dev),
        out_shape=jax.ShapeDtypeStruct(total.shape, jnp.float32),
        in_specs=[in_vmem, in_vmem, in_vmem, in_place],
        out_specs=in_place,
        input_output_aliases={3: 0},
        scratch_shapes=[
            pltpu.VMEM((width, columns), jnp.float32),
            pltpu.SemaphoreType.DMA((2,)),
        ],
        compiler_params=pltpu.CompilerParams(vmem_limit_bytes=12 << 20),
        name="last",
    )(elim, partial, arrived, total)


def local(design, arc_partials, arc_id, arc_weight):
    row_count, col_count = lax.axis_size("row"), lax.axis_size("col")
    held, elim, ready, piece = gather(design, arc_partials, arc_id, arc_weight, row_count, col_count)
    arrived = lax.ppermute(piece, "col", [(1, 0), (col_count - 2, col_count - 1)])
    total, partial = finish(held, elim, ready)
    return last(elim, partial, arrived, total, design.shape[0])


def solution(mesh):
    placed = (P(("row", "col"), None), P(("row", "col"), None, None), P(("row", "col")), P())
    return jax.shard_map(
        local, mesh=mesh, in_specs=placed, out_specs=P("row", "col"), check_vma=False
    )
```

```python
import functools

import jax
import jax.numpy as jnp
from jax import lax
from jax.experimental import pallas as pl
from jax.experimental.pallas import tpu as pltpu
from jax.sharding import PartitionSpec as P

SLAB = 2048
LANES = 128
GROUP = 8
RIDGE = 4.0
SKEW = 1
AHEAD = 3
FACTS_STEP = 3
SOLVE_AFTER = 3
LEFT = 2

MESH = pl.DeviceIdType.MESH
HIGH = lax.Precision.HIGHEST


def chunk_width(rows):
    blocks = rows // LANES
    return LANES * max(k for k in range(1, 9) if blocks % k == 0)


def partner(r, p, count):
    out, bit = 0, 1
    while bit < count:
        out = out + bit * lax.rem(r // bit + p // bit, 2)
        bit *= 2
    return out


def dot(a, b, dims):
    return lax.dot_general(a, b, (dims, ((), ())), precision=HIGH, preferred_element_type=jnp.float32)


def eliminate(facts, values, order, arcs, rows_dev):
    wide = -(-arcs * GROUP // LANES) * LANES
    lane_in = lax.broadcasted_iota(jnp.int32, (LANES, wide), 0)
    lane_out = lax.broadcasted_iota(jnp.int32, (LANES, wide), 1)
    repeat = (lane_in // rows_dev == lane_out % GROUP).astype(jnp.float32)
    epoch = lax.broadcasted_iota(jnp.int32, facts.shape, 0)
    lane = lax.broadcasted_iota(jnp.int32, facts.shape, 1)
    own = (lane % rows_dev == epoch % rows_dev) & (lane < order * rows_dev)
    partials = dot(jnp.where(own, facts, 0.0), repeat, ((1,), (0,)))
    arc = (lax.broadcasted_iota(jnp.int32, partials.shape, 1) // GROUP).astype(jnp.float32)
    at_id = order * rows_dev
    spread = jnp.where(facts[:, at_id : at_id + 1] == arc, partials, 0.0)
    rhs = dot(spread, values, ((0,), (0,))).reshape(wide // GROUP, GROUP, -1)
    gram = dot(spread, partials[:, 0:LANES], ((0,), (0,))).reshape(wide // GROUP, GROUP, LANES)
    at = lax.broadcasted_iota(jnp.int32, gram.shape, 1)
    gram = gram + jnp.where(at == lax.broadcasted_iota(jnp.int32, gram.shape, 2), RIDGE, 0.0)
    at_rhs = lax.broadcasted_iota(jnp.int32, rhs.shape, 1)
    for pivot in range(order):
        scale = 1.0 / gram[:, pivot : pivot + 1, pivot : pivot + 1]
        row_gram = gram[:, pivot : pivot + 1, :] * scale
        row_rhs = rhs[:, pivot : pivot + 1, :] * scale
        factor = gram[:, :, pivot : pivot + 1]
        gram = jnp.where(at == pivot, row_gram, gram - factor * row_gram)
        rhs = jnp.where(at_rhs == pivot, row_rhs, rhs - factor * row_rhs)
    fitted = dot(spread, rhs.reshape(wide, -1), ((1,), (0,)))
    return (facts[:, at_id + 1 : at_id + 2] * (values - fitted)).astype(jnp.bfloat16)


def product_tile(held, elim, start, tile):
    epochs = elim.shape[0] * elim.shape[1]
    return (1.0 / epochs) * lax.dot_general(
        held[:, :, pl.ds(pl.multiple_of(start, tile), tile)].reshape(epochs, tile),
        elim[...].reshape(epochs, -1),
        (((0,), (0,)), ((), ())),
        preferred_element_type=jnp.float32,
    )


def gather_kernel(
    row_count, col_count, width,
    design, partials_in, ids, weights_in,
    held, elim, ready, piece,
    slab, facts, spread_facts, partials, weights,
    recv_z, own_down, own_up, send_down, send_up, recv_in, send_in, own_sem,
    slab_sem, facts_sem,
):
    r, c = lax.axis_index("row"), lax.axis_index("col")
    rows_dev, coefficients = design.shape
    rows = coefficients // row_count
    block = row_count * rows_dev
    columns = slab.shape[2]
    order, arcs = partials.shape[0], weights.shape[0]
    chunks = rows // width
    slab_chunks = -(-columns * col_count // width)
    peers = [partner(r, p, row_count) for p in range(row_count)]

    barrier = pltpu.get_barrier_semaphore()
    for p in range(1, row_count):
        pl.semaphore_signal(barrier, inc=1, device_id=(peers[p], c), device_id_type=MESH)
    for k in range(1, col_count):
        pl.semaphore_signal(barrier, inc=1, device_id=(r, lax.rem(c + k, col_count)), device_id_type=MESH)
    pl.semaphore_wait(barrier, row_count + col_count - 2)

    def remote(src, dst, send, recv, device):
        return pltpu.make_async_remote_copy(
            src_ref=src, dst_ref=dst, send_sem=send, recv_sem=recv, device_id=device, device_id_type=MESH
        )

    def arrived(ref, sem):
        pltpu.make_async_copy(ref, ref, sem).wait()

    def own_block(z):
        return held.at[z, pl.ds(0, rows_dev), :]

    def part(j):
        return pl.ds(pl.multiple_of(j * width, width), width)

    def chunk(z, j):
        return held.at[z, pl.ds(rows_dev, block - rows_dev), part(j)]

    mine = design.at[:, pl.ds(pl.multiple_of(r * rows, LANES), rows)]
    down, up = (r, lax.max(c - 1, 0)), (r, lax.min(c + 1, col_count - 1))

    @pl.when(c > 0)
    def _():
        remote(mine, own_block(c), own_down.at[c], recv_z.at[c, 0], down).start()

    @pl.when(c < col_count - 1)
    def _():
        remote(mine, own_block(c), own_up.at[c], recv_z.at[c, 0], up).start()

    def send_chunk(j):
        for p in range(1, row_count):
            start = pl.multiple_of(peers[p] * rows + j * width, LANES)
            remote(
                design.at[:, pl.ds(start, width)],
                held.at[c, pl.ds(p * rows_dev, rows_dev), part(j)],
                send_in.at[0],
                recv_in.at[j],
                (peers[p], c),
            ).start()

    small = [
        pltpu.make_async_copy(src, dst, own_sem.at[1 + i])
        for i, (src, dst) in enumerate(((partials_in, partials), (weights_in, weights)))
    ]
    for copy in small:
        copy.start()
    for j in range(min(AHEAD, chunks)):
        send_chunk(j)
    own_copy = pltpu.make_async_copy(mine, own_block(c), own_sem.at[0])
    own_copy.start()

    for copy in small:
        copy.wait()
    lane = lax.broadcasted_iota(jnp.int32, (1, LANES), 1)
    row = jnp.where(lane == order * rows_dev, ids[0].astype(jnp.float32), 0.0)
    row = jnp.where(lane == order * rows_dev + 1, weights[ids[0]], row)
    shift_in = lax.broadcasted_iota(jnp.int32, (rows_dev, LANES), 0)
    shift_out = lax.broadcasted_iota(jnp.int32, (rows_dev, LANES), 1)
    for p in range(order):
        place = (shift_out == shift_in + p * rows_dev).astype(jnp.float32)
        row = row + dot(partials[p], place, ((1,), (0,)))
    facts[c, r] = row
    mine_facts = facts.at[c, r]
    for k in range(1, col_count):
        other = lax.rem(c + k, col_count)
        remote(mine_facts, mine_facts, facts_sem.at[0], facts_sem.at[1], (r, other)).start()
    others = facts.at[pl.ds(0, col_count - 1), 0]
    rest = facts.at[:, pl.ds(0, row_count - 1)]

    def step(t, _):
        @pl.when((t + AHEAD - 1 < chunks) & (t >= 1))
        def _():
            send_chunk(t + AHEAD - 1)

        @pl.when((t >= 1) & (t <= chunks))
        def _():
            own = chunk(c, t - 1)
            arrived(own, recv_in.at[t - 1])

            @pl.when(c > 0)
            def _():
                remote(own, own, send_down.at[c], recv_z.at[c, t], down).start()

            @pl.when(c < col_count - 1)
            def _():
                remote(own, own, send_up.at[c], recv_z.at[c, t], up).start()

        for d in range(1, col_count):
            unit = t - d * SKEW
            for z, exists, onward, own_sems, sems, target in (
                (c + d, c + d < col_count, c > 0, own_down, send_down, down),
                (c - d, c - d >= 0, c < col_count - 1, own_up, send_up, up),
            ):

                @pl.when((unit == 0) & exists)
                def _():
                    ref = own_block(z)
                    arrived(ref, recv_z.at[z, 0])

                    @pl.when(onward)
                    def _():
                        remote(ref, ref, own_sems.at[z], recv_z.at[z, 0], target).start()

                units = chunks if d < col_count - 1 else chunks - 1

                @pl.when((unit >= 1) & (unit <= units) & exists)
                def _():
                    ref = chunk(z, unit - 1)
                    arrived(ref, recv_z.at[z, unit])
                    sends = onward if d < col_count - 2 else onward & (unit < chunks)

                    @pl.when(sends)
                    def _():
                        remote(ref, ref, sems.at[z], recv_z.at[z, unit], target).start()

                    if d == col_count - 2:

                        @pl.when(onward & (unit == chunks))
                        def _():
                            pltpu.make_async_copy(ref, piece, own_sem.at[3]).start()

        @pl.when(t == FACTS_STEP)
        def _():
            arrived(others, facts_sem.at[1])
            for p in range(1, row_count):
                ref = facts.at[:, r]
                remote(ref, ref, facts_sem.at[2], facts_sem.at[3], (peers[p], c)).start()

        @pl.when((t == slab_step) & (r == 0))
        def _():
            own_copy.wait()
            source = held.at[:, :, pl.ds(pl.multiple_of(c * columns, columns), columns)]
            for p in range(1, row_count):
                remote(source, slab, slab_sem.at[0], slab_sem.at[1], (p, c)).start()
            local_slab = pltpu.make_async_copy(source, slab, slab_sem.at[2])
            local_slab.start()
            local_slab.wait()

        @pl.when(t == solve_step)
        def _():
            @pl.when(r > 0)
            def _():
                own_copy.wait()
                arrived(slab, slab_sem.at[1])

            arrived(rest, facts_sem.at[3])
            for z in range(col_count):
                for k in range(row_count):
                    spread_facts[pl.ds((z * row_count + k) * rows_dev, rows_dev), :] = jnp.broadcast_to(
                        facts[z, k], (rows_dev, LANES)
                    )
            out = eliminate(
                spread_facts[...],
                slab[...].reshape(col_count * block, columns).astype(jnp.float32),
                order,
                arcs,
                rows_dev,
            ).reshape(col_count, block, columns)
            for edge, far in ((0, col_count - 1), (col_count - 1, 0)):

                @pl.when(c == edge)
                def _():
                    piece[...] = jnp.zeros_like(piece)
                    held[far, rows_dev:block, rows - width : rows] = jnp.zeros(
                        (block - rows_dev, width), jnp.bfloat16
                    )

            for k in range(row_count):
                at = pl.ds(pl.multiple_of(peers[k] * rows_dev, rows_dev), rows_dev)
                elim[:, at, :] = out[:, k * rows_dev : (k + 1) * rows_dev, :]

        here = lax.min(lax.max(t - (col_count - 1) * SKEW, 0), chunks - LEFT)
        before = lax.min(lax.max(t - 1 - (col_count - 1) * SKEW, 0), chunks - LEFT)

        @pl.when(t >= solve_step)
        def _():
            def form(j, _):
                ready[part(j), :] = product_tile(held, elim, j * width, width)
                return 0

            lax.fori_loop(lax.select(t == solve_step, 0, before), here, form, 0)

        return 0

    slab_step = slab_chunks + (col_count - 1) * SKEW
    solve_step = slab_step + SOLVE_AFTER
    lax.fori_loop(0, chunks + 1 + (col_count - 1) * SKEW, step, 0)

    sent = design.at[:, pl.ds(0, (row_count - 1) * rows)]
    arrived(sent, send_in.at[0])
    arrived(others, facts_sem.at[0])
    arrived(rest, facts_sem.at[2])

    @pl.when(r == 0)
    def _():
        share = held.at[:, :, pl.ds(0, (row_count - 1) * columns)]
        arrived(share, slab_sem.at[0])

    for z in range(col_count):
        others_of = held.at[z, pl.ds(rows_dev, block - rows_dev), :]
        shorter = held.at[z, pl.ds(rows_dev, block - rows_dev), pl.ds(0, rows - width)]
        for sends, far, last_hop, own_sems, sems in (
            ((c > 0) & (z >= c), col_count - 1, c == 1, own_down, send_down),
            ((c < col_count - 1) & (z <= c), 0, c == col_count - 2, own_up, send_up),
        ):

            @pl.when(sends)
            def _():
                arrived(own_block(z), own_sems.at[z])

            if z == far:

                @pl.when(sends & last_hop)
                def _():
                    arrived(shorter, sems.at[z])
                    arrived(piece, own_sem.at[3])

                sends = sends & jnp.logical_not(last_hop)

            @pl.when(sends)
            def _():
                arrived(others_of, sems.at[z])


def in_hbm(array):
    return pltpu.with_memory_space_constraint(array, pltpu.HBM)


def gather(design, arc_partials, arc_id, arc_weight, row_count, col_count):
    rows_dev, coefficients = design.shape
    rows = coefficients // row_count
    columns = SLAB // col_count
    block = rows_dev * row_count
    width = chunk_width(rows)
    chunks = rows // width
    dma = pltpu.SemaphoreType.DMA
    partials = arc_partials.transpose(1, 0, 2)
    in_vmem = pl.BlockSpec(memory_space=pltpu.VMEM)
    return pl.pallas_call(
        functools.partial(gather_kernel, row_count, col_count, width),
        out_shape=(
            pltpu.VMEM((col_count, block, rows), jnp.bfloat16),
            pltpu.VMEM((col_count, block, columns), jnp.bfloat16),
            pltpu.VMEM((rows - LEFT * width, columns), jnp.float32),
            pltpu.VMEM((block - rows_dev, width), jnp.bfloat16),
        ),
        in_specs=[
            pl.BlockSpec(memory_space=pltpu.HBM),
            pl.BlockSpec(memory_space=pltpu.HBM),
            pl.BlockSpec(memory_space=pltpu.SMEM),
            pl.BlockSpec(memory_space=pltpu.HBM),
        ],
        out_specs=(in_vmem,) * 4,
        scratch_shapes=[
            pltpu.VMEM((col_count, block, columns), jnp.bfloat16),
            pltpu.VMEM((col_count, row_count, 1, LANES), jnp.float32),
            pltpu.VMEM((col_count * block, LANES), jnp.float32),
            pltpu.VMEM(partials.shape, jnp.float32),
            pltpu.SMEM(arc_weight.shape, jnp.float32),
            dma((col_count, chunks + 1)),
            dma((col_count,)),
            dma((col_count,)),
            dma((col_count,)),
            dma((col_count,)),
            dma((chunks,)),
            dma((1,)),
            dma((4,)),
            dma((3,)),
            dma((4,)),
        ],
        compiler_params=pltpu.CompilerParams(
            collective_id=0, has_side_effects=True, vmem_limit_bytes=16 << 20
        ),
        name="gather",
    )(in_hbm(design), in_hbm(partials), arc_id, in_hbm(arc_weight))


def finish_kernel(held, elim, ready, out, partial, tile, sems):
    size = partial.shape[0]
    count = ready.shape[0] // size

    def copy(i):
        at = pl.ds(i * size, size)
        source = ready.at[at, :] if i < count else tile.at[i - count]
        return pltpu.make_async_copy(source, out.at[at, :], sems.at[i])

    for i in range(count):
        copy(i).start()
    for i in range(count, count + LEFT - 1):
        tile[i - count] = product_tile(held, elim, i * size, size)
        copy(i).start()
    partial[...] = product_tile(held, elim, (count + LEFT - 1) * size, size)
    for i in range(count + LEFT - 1):
        copy(i).wait()


def finish(held, elim, ready):
    col_count, block, rows = held.shape
    columns = elim.shape[2]
    width = chunk_width(rows)
    in_vmem = pl.BlockSpec(memory_space=pltpu.VMEM)
    return pl.pallas_call(
        finish_kernel,
        out_shape=(
            jax.ShapeDtypeStruct((rows, columns), jnp.float32),
            pltpu.VMEM((width, columns), jnp.float32),
        ),
        in_specs=[in_vmem, in_vmem, in_vmem],
        out_specs=(pl.BlockSpec(memory_space=pl.ANY), in_vmem),
        scratch_shapes=[
            pltpu.VMEM((LEFT - 1, width, columns), jnp.float32),
            pltpu.SemaphoreType.DMA((rows // width - 1,)),
        ],
        compiler_params=pltpu.CompilerParams(vmem_limit_bytes=12 << 20),
        cost_estimate=pl.CostEstimate(
            flops=2 * LEFT * col_count * block * width * columns,
            bytes_accessed=4 * rows * columns,
            transcendentals=0,
        ),
        name="finish",
    )(held, elim, ready)


def last_kernel(scale, rows_dev, elim, partial, arrived, total, out, tile, sems):
    col_count, block, _ = elim.shape
    width = partial.shape[0]
    half = width // 2
    far = lax.select(lax.axis_index("col") == 0, col_count - 1, 0)
    copies = []
    for i in range(2):
        at = pl.ds(i * half, half)
        tile[at, :] = partial[at, :] + scale * lax.dot_general(
            arrived[:, at],
            elim[far, rows_dev:block, :],
            (((0,), (0,)), ((), ())),
            preferred_element_type=jnp.float32,
        )
        to = pl.ds(out.shape[0] - width + i * half, half)
        copies.append(pltpu.make_async_copy(tile.at[at, :], out.at[to, :], sems.at[i]))
        copies[i].start()
    for copy in copies:
        copy.wait()


def last(elim, partial, arrived, total, rows_dev):
    col_count, block, columns = elim.shape
    width = partial.shape[0]
    in_vmem = pl.BlockSpec(memory_space=pltpu.VMEM)
    in_place = pl.BlockSpec(memory_space=pl.ANY)
    return pl.pallas_call(
        functools.partial(last_kernel, 1.0 / (col_count * block), rows_dev),
        out_shape=jax.ShapeDtypeStruct(total.shape, jnp.float32),
        in_specs=[in_vmem, in_vmem, in_vmem, in_place],
        out_specs=in_place,
        input_output_aliases={3: 0},
        scratch_shapes=[
            pltpu.VMEM((width, columns), jnp.float32),
            pltpu.SemaphoreType.DMA((2,)),
        ],
        compiler_params=pltpu.CompilerParams(vmem_limit_bytes=12 << 20),
        name="last",
    )(elim, partial, arrived, total)


def local(design, arc_partials, arc_id, arc_weight):
    row_count, col_count = lax.axis_size("row"), lax.axis_size("col")
    held, elim, ready, piece = gather(design, arc_partials, arc_id, arc_weight, row_count, col_count)
    pairs = [(1, 0), (0, 1), (col_count - 2, col_count - 1), (col_count - 1, col_count - 2)]
    arrived = lax.ppermute(piece, "col", pairs)
    total, partial = finish(held, elim, ready)
    return last(elim, partial, arrived, total, design.shape[0])


def solution(mesh):
    placed = (P(("row", "col"), None), P(("row", "col"), None, None), P(("row", "col")), P())
    return jax.shard_map(
        local, mesh=mesh, in_specs=placed, out_specs=P("row", "col"), check_vma=False
    )
```

```python
import functools

import jax
import jax.numpy as jnp
from jax import lax
from jax.experimental import pallas as pl
from jax.experimental.pallas import tpu as pltpu
from jax.sharding import PartitionSpec as P

SLAB = 2048
LANES = 128
GROUP = 8
RIDGE = 4.0
SKEW = 1
AHEAD = 3
FACTS_STEP = 3
SOLVE_AFTER = 3
LEFT = 2

MESH = pl.DeviceIdType.MESH
HIGH = lax.Precision.HIGHEST


def chunk_width(rows):
    blocks = rows // LANES
    return LANES * max(k for k in range(1, 9) if blocks % k == 0)


def narrow_width(width, col_count):
    return LANES * -(-(width // LANES) // (col_count - 1))


def partner(r, p, count):
    out, bit = 0, 1
    while bit < count:
        out = out + bit * lax.rem(r // bit + p // bit, 2)
        bit *= 2
    return out


def dot(a, b, dims):
    return lax.dot_general(a, b, (dims, ((), ())), precision=HIGH, preferred_element_type=jnp.float32)


def eliminate(facts, values, order, arcs, rows_dev):
    wide = -(-arcs * GROUP // LANES) * LANES
    lane_in = lax.broadcasted_iota(jnp.int32, (LANES, wide), 0)
    lane_out = lax.broadcasted_iota(jnp.int32, (LANES, wide), 1)
    repeat = (lane_in // rows_dev == lane_out % GROUP).astype(jnp.float32)
    epoch = lax.broadcasted_iota(jnp.int32, facts.shape, 0)
    lane = lax.broadcasted_iota(jnp.int32, facts.shape, 1)
    own = (lane % rows_dev == epoch % rows_dev) & (lane < order * rows_dev)
    partials = dot(jnp.where(own, facts, 0.0), repeat, ((1,), (0,)))
    arc = (lax.broadcasted_iota(jnp.int32, partials.shape, 1) // GROUP).astype(jnp.float32)
    at_id = order * rows_dev
    spread = jnp.where(facts[:, at_id : at_id + 1] == arc, partials, 0.0)
    rhs = dot(spread, values, ((0,), (0,))).reshape(wide // GROUP, GROUP, -1)
    gram = dot(spread, partials[:, 0:LANES], ((0,), (0,))).reshape(wide // GROUP, GROUP, LANES)
    at = lax.broadcasted_iota(jnp.int32, gram.shape, 1)
    gram = gram + jnp.where(at == lax.broadcasted_iota(jnp.int32, gram.shape, 2), RIDGE, 0.0)
    at_rhs = lax.broadcasted_iota(jnp.int32, rhs.shape, 1)
    for pivot in range(order):
        scale = 1.0 / gram[:, pivot : pivot + 1, pivot : pivot + 1]
        row_gram = gram[:, pivot : pivot + 1, :] * scale
        row_rhs = rhs[:, pivot : pivot + 1, :] * scale
        factor = gram[:, :, pivot : pivot + 1]
        gram = jnp.where(at == pivot, row_gram, gram - factor * row_gram)
        rhs = jnp.where(at_rhs == pivot, row_rhs, rhs - factor * row_rhs)
    fitted = dot(spread, rhs.reshape(wide, -1), ((1,), (0,)))
    return (facts[:, at_id + 1 : at_id + 2] * (values - fitted)).astype(jnp.bfloat16)


def product_tile(held, elim, start, tile):
    epochs = elim.shape[0] * elim.shape[1]
    return (1.0 / epochs) * lax.dot_general(
        held[:, :, pl.ds(pl.multiple_of(start, LANES), tile)].reshape(epochs, tile),
        elim[...].reshape(epochs, -1),
        (((0,), (0,)), ((), ())),
        preferred_element_type=jnp.float32,
    )


def gather_kernel(
    row_count, col_count, width,
    design, partials_in, ids, weights_in,
    held, elim, ready, piece,
    slab, facts, spread_facts, partials, weights,
    recv_z, own_down, own_up, send_down, send_up, recv_in, send_in, own_sem,
    slab_sem, facts_sem,
):
    r, c = lax.axis_index("row"), lax.axis_index("col")
    rows_dev, coefficients = design.shape
    rows = coefficients // row_count
    block = row_count * rows_dev
    columns = slab.shape[2]
    order, arcs = partials.shape[0], weights.shape[0]
    chunks = rows // width
    slab_chunks = -(-columns * col_count // width)
    peers = [partner(r, p, row_count) for p in range(row_count)]

    barrier = pltpu.get_barrier_semaphore()
    for p in range(1, row_count):
        pl.semaphore_signal(barrier, inc=1, device_id=(peers[p], c), device_id_type=MESH)
    for k in range(1, col_count):
        pl.semaphore_signal(barrier, inc=1, device_id=(r, lax.rem(c + k, col_count)), device_id_type=MESH)
    pl.semaphore_wait(barrier, row_count + col_count - 2)

    def remote(src, dst, send, recv, device):
        return pltpu.make_async_remote_copy(
            src_ref=src, dst_ref=dst, send_sem=send, recv_sem=recv, device_id=device, device_id_type=MESH
        )

    def arrived(ref, sem):
        pltpu.make_async_copy(ref, ref, sem).wait()

    def own_block(z):
        return held.at[z, pl.ds(0, rows_dev), :]

    def part(j):
        return pl.ds(pl.multiple_of(j * width, width), width)

    def chunk(z, j):
        return held.at[z, pl.ds(rows_dev, block - rows_dev), part(j)]

    narrow = narrow_width(width, col_count)
    others = pl.ds(rows_dev, block - rows_dev)

    def early(z):
        return held.at[z, others, pl.ds(rows - width, width - narrow)]

    def forward(z, unit, sems, target, last_hop, k):
        cut = last_hop & (unit == chunks)

        @pl.when(jnp.logical_not(cut))
        def _():
            ref = chunk(z, unit - 1)
            remote(ref, ref, sems.at[z], recv_z.at[z, unit], target).start()

        @pl.when(cut)
        def _():
            remote(early(z), early(z), sems.at[z], recv_z.at[z, unit], target).start()
            late = held.at[z, others, pl.ds(rows - narrow, narrow)]
            pltpu.make_async_copy(late, piece.at[k], own_sem.at[3]).start()

    before_low, before_high = c == 1, c == col_count - 2
    mine = design.at[:, pl.ds(pl.multiple_of(r * rows, LANES), rows)]
    down, up = (r, lax.max(c - 1, 0)), (r, lax.min(c + 1, col_count - 1))

    @pl.when(c > 0)
    def _():
        remote(mine, own_block(c), own_down.at[c], recv_z.at[c, 0], down).start()

    @pl.when(c < col_count - 1)
    def _():
        remote(mine, own_block(c), own_up.at[c], recv_z.at[c, 0], up).start()

    def send_chunk(j):
        for p in range(1, row_count):
            start = pl.multiple_of(peers[p] * rows + j * width, LANES)
            remote(
                design.at[:, pl.ds(start, width)],
                held.at[c, pl.ds(p * rows_dev, rows_dev), part(j)],
                send_in.at[0],
                recv_in.at[j],
                (peers[p], c),
            ).start()

    small = [
        pltpu.make_async_copy(src, dst, own_sem.at[1 + i])
        for i, (src, dst) in enumerate(((partials_in, partials), (weights_in, weights)))
    ]
    for copy in small:
        copy.start()
    for j in range(min(AHEAD, chunks)):
        send_chunk(j)
    own_copy = pltpu.make_async_copy(mine, own_block(c), own_sem.at[0])
    own_copy.start()

    for copy in small:
        copy.wait()
    lane = lax.broadcasted_iota(jnp.int32, (1, LANES), 1)
    row = jnp.where(lane == order * rows_dev, ids[0].astype(jnp.float32), 0.0)
    row = jnp.where(lane == order * rows_dev + 1, weights[ids[0]], row)
    shift_in = lax.broadcasted_iota(jnp.int32, (rows_dev, LANES), 0)
    shift_out = lax.broadcasted_iota(jnp.int32, (rows_dev, LANES), 1)
    for p in range(order):
        place = (shift_out == shift_in + p * rows_dev).astype(jnp.float32)
        row = row + dot(partials[p], place, ((1,), (0,)))
    facts[c, r] = row
    mine_facts = facts.at[c, r]
    for k in range(1, col_count):
        other = lax.rem(c + k, col_count)
        remote(mine_facts, mine_facts, facts_sem.at[0], facts_sem.at[1], (r, other)).start()
    other_facts = facts.at[pl.ds(0, col_count - 1), 0]
    rest = facts.at[:, pl.ds(0, row_count - 1)]

    def step(t, _):
        @pl.when((t + AHEAD - 1 < chunks) & (t >= 1))
        def _():
            send_chunk(t + AHEAD - 1)

        @pl.when((t >= 1) & (t <= chunks))
        def _():
            own = chunk(c, t - 1)
            arrived(own, recv_in.at[t - 1])

            @pl.when(c > 0)
            def _():
                forward(c, t, send_down, down, before_low, c - 1)

            @pl.when(c < col_count - 1)
            def _():
                forward(c, t, send_up, up, before_high, c)

        for d in range(1, col_count):
            unit = t - d * SKEW
            for z, k, exists, onward, last_hop, own_sems, sems, target in (
                (c + d, c + d - 1, c + d < col_count, c > 0, before_low, own_down, send_down, down),
                (c - d, c - d, c - d >= 0, c < col_count - 1, before_high, own_up, send_up, up),
            ):

                @pl.when((unit == 0) & exists)
                def _():
                    ref = own_block(z)
                    arrived(ref, recv_z.at[z, 0])

                    @pl.when(onward)
                    def _():
                        remote(ref, ref, own_sems.at[z], recv_z.at[z, 0], target).start()

                @pl.when((unit >= 1) & exists & ((unit < chunks) | (onward & (unit == chunks))))
                def _():
                    arrived(chunk(z, unit - 1), recv_z.at[z, unit])

                    @pl.when(onward)
                    def _():
                        forward(z, unit, sems, target, last_hop, k)

                @pl.when((unit == chunks) & exists & jnp.logical_not(onward))
                def _():
                    arrived(early(z), recv_z.at[z, unit])

        @pl.when(t == FACTS_STEP)
        def _():
            arrived(other_facts, facts_sem.at[1])
            for p in range(1, row_count):
                ref = facts.at[:, r]
                remote(ref, ref, facts_sem.at[2], facts_sem.at[3], (peers[p], c)).start()

        @pl.when((t == slab_step) & (r == 0))
        def _():
            own_copy.wait()
            source = held.at[:, :, pl.ds(pl.multiple_of(c * columns, columns), columns)]
            for p in range(1, row_count):
                remote(source, slab, slab_sem.at[0], slab_sem.at[1], (p, c)).start()
            local_slab = pltpu.make_async_copy(source, slab, slab_sem.at[2])
            local_slab.start()
            local_slab.wait()

        @pl.when(t == solve_step)
        def _():
            @pl.when(r > 0)
            def _():
                own_copy.wait()
                arrived(slab, slab_sem.at[1])

            arrived(rest, facts_sem.at[3])
            for z in range(col_count):
                for k in range(row_count):
                    spread_facts[pl.ds((z * row_count + k) * rows_dev, rows_dev), :] = jnp.broadcast_to(
                        facts[z, k], (rows_dev, LANES)
                    )
            out = eliminate(
                spread_facts[...],
                slab[...].reshape(col_count * block, columns).astype(jnp.float32),
                order,
                arcs,
                rows_dev,
            ).reshape(col_count, block, columns)
            for edge, first in ((0, 1), (col_count - 1, 0)):

                @pl.when(c == edge)
                def _():
                    piece[...] = jnp.zeros_like(piece)
                    for z in range(first, first + col_count - 1):
                        held[z, rows_dev:block, rows - narrow : rows] = jnp.zeros(
                            (block - rows_dev, narrow), jnp.bfloat16
                        )

            for k in range(row_count):
                at = pl.ds(pl.multiple_of(peers[k] * rows_dev, rows_dev), rows_dev)
                elim[:, at, :] = out[:, k * rows_dev : (k + 1) * rows_dev, :]

        here = lax.min(lax.max(t - (col_count - 1) * SKEW, 0), chunks - LEFT)
        before = lax.min(lax.max(t - 1 - (col_count - 1) * SKEW, 0), chunks - LEFT)

        @pl.when(t >= solve_step)
        def _():
            def form(j, _):
                ready[part(j), :] = product_tile(held, elim, j * width, width)
                return 0

            lax.fori_loop(lax.select(t == solve_step, 0, before), here, form, 0)

        return 0

    slab_step = slab_chunks + (col_count - 1) * SKEW
    solve_step = slab_step + SOLVE_AFTER
    lax.fori_loop(0, chunks + 1 + (col_count - 1) * SKEW, step, 0)

    sent = design.at[:, pl.ds(0, (row_count - 1) * rows)]
    arrived(sent, send_in.at[0])
    arrived(other_facts, facts_sem.at[0])
    arrived(rest, facts_sem.at[2])

    @pl.when(r == 0)
    def _():
        share = held.at[:, :, pl.ds(0, (row_count - 1) * columns)]
        arrived(share, slab_sem.at[0])

    for z in range(col_count):
        for sends, last_hop, own_sems, sems in (
            ((c > 0) & (z >= c), before_low, own_down, send_down),
            ((c < col_count - 1) & (z <= c), before_high, own_up, send_up),
        ):

            @pl.when(sends)
            def _():
                arrived(own_block(z), own_sems.at[z])

            @pl.when(sends & last_hop)
            def _():
                arrived(held.at[z, others, pl.ds(0, rows - narrow)], sems.at[z])

            @pl.when(sends & jnp.logical_not(last_hop))
            def _():
                arrived(held.at[z, others, :], sems.at[z])

    @pl.when(before_low | before_high)
    def _():
        arrived(piece, own_sem.at[3])


def in_hbm(array):
    return pltpu.with_memory_space_constraint(array, pltpu.HBM)


def gather(design, arc_partials, arc_id, arc_weight, row_count, col_count):
    rows_dev, coefficients = design.shape
    rows = coefficients // row_count
    columns = SLAB // col_count
    block = rows_dev * row_count
    width = chunk_width(rows)
    chunks = rows // width
    dma = pltpu.SemaphoreType.DMA
    partials = arc_partials.transpose(1, 0, 2)
    in_vmem = pl.BlockSpec(memory_space=pltpu.VMEM)
    return pl.pallas_call(
        functools.partial(gather_kernel, row_count, col_count, width),
        out_shape=(
            pltpu.VMEM((col_count, block, rows), jnp.bfloat16),
            pltpu.VMEM((col_count, block, columns), jnp.bfloat16),
            pltpu.VMEM((rows - LEFT * width, columns), jnp.float32),
            pltpu.VMEM((col_count - 1, block - rows_dev, narrow_width(width, col_count)), jnp.bfloat16),
        ),
        in_specs=[
            pl.BlockSpec(memory_space=pltpu.HBM),
            pl.BlockSpec(memory_space=pltpu.HBM),
            pl.BlockSpec(memory_space=pltpu.SMEM),
            pl.BlockSpec(memory_space=pltpu.HBM),
        ],
        out_specs=(in_vmem,) * 4,
        scratch_shapes=[
            pltpu.VMEM((col_count, block, columns), jnp.bfloat16),
            pltpu.VMEM((col_count, row_count, 1, LANES), jnp.float32),
            pltpu.VMEM((col_count * block, LANES), jnp.float32),
            pltpu.VMEM(partials.shape, jnp.float32),
            pltpu.SMEM(arc_weight.shape, jnp.float32),
            dma((col_count, chunks + 1)),
            dma((col_count,)),
            dma((col_count,)),
            dma((col_count,)),
            dma((col_count,)),
            dma((chunks,)),
            dma((1,)),
            dma((4,)),
            dma((3,)),
            dma((4,)),
        ],
        compiler_params=pltpu.CompilerParams(
            collective_id=0, has_side_effects=True, vmem_limit_bytes=16 << 20
        ),
        name="gather",
    )(in_hbm(design), in_hbm(partials), arc_id, in_hbm(arc_weight))


def finish_kernel(size, held, elim, ready, out, partial, tile, sems):
    rows = out.shape[0]
    count = ready.shape[0] // size
    narrow = partial.shape[0]
    copies = [
        pltpu.make_async_copy(ready.at[at, :], out.at[at, :], sems.at[i])
        for i, at in enumerate(pl.ds(i * size, size) for i in range(count))
    ]
    for copy in copies:
        copy.start()
    for k, (start, length) in enumerate(((rows - LEFT * size, size), (rows - size, size - narrow))):
        tile[k, 0:length, :] = product_tile(held, elim, start, length)
        to = out.at[pl.ds(start, length), :]
        copies.append(pltpu.make_async_copy(tile.at[k, pl.ds(0, length), :], to, sems.at[count + k]))
        copies[-1].start()
    partial[...] = product_tile(held, elim, rows - narrow, narrow)
    for copy in copies:
        copy.wait()


def finish(held, elim, ready):
    col_count, block, rows = held.shape
    columns = elim.shape[2]
    width = chunk_width(rows)
    in_vmem = pl.BlockSpec(memory_space=pltpu.VMEM)
    return pl.pallas_call(
        functools.partial(finish_kernel, width),
        out_shape=(
            jax.ShapeDtypeStruct((rows, columns), jnp.float32),
            pltpu.VMEM((narrow_width(width, col_count), columns), jnp.float32),
        ),
        in_specs=[in_vmem, in_vmem, in_vmem],
        out_specs=(pl.BlockSpec(memory_space=pl.ANY), in_vmem),
        scratch_shapes=[
            pltpu.VMEM((LEFT, width, columns), jnp.float32),
            pltpu.SemaphoreType.DMA((rows // width,)),
        ],
        compiler_params=pltpu.CompilerParams(vmem_limit_bytes=12 << 20),
        cost_estimate=pl.CostEstimate(
            flops=2 * LEFT * col_count * block * width * columns,
            bytes_accessed=4 * rows * columns,
            transcendentals=0,
        ),
        name="finish",
    )(held, elim, ready)


def last_kernel(scale, rows_dev, elim, partial, arrived, total, out, tile, sem):
    col_count, block, _ = elim.shape
    narrow = partial.shape[0]
    first = lax.select(lax.axis_index("col") == 0, 1, 0)
    value = partial[...]
    for k in range(col_count - 1):
        value = value + scale * lax.dot_general(
            arrived[k],
            elim[first + k, rows_dev:block, :],
            (((0,), (0,)), ((), ())),
            preferred_element_type=jnp.float32,
        )
    tile[...] = value
    copy = pltpu.make_async_copy(tile, out.at[pl.ds(out.shape[0] - narrow, narrow), :], sem)
    copy.start()
    copy.wait()


def last(elim, partial, arrived, total, rows_dev):
    col_count, block, columns = elim.shape
    in_vmem = pl.BlockSpec(memory_space=pltpu.VMEM)
    in_place = pl.BlockSpec(memory_space=pl.ANY)
    return pl.pallas_call(
        functools.partial(last_kernel, 1.0 / (col_count * block), rows_dev),
        out_shape=jax.ShapeDtypeStruct(total.shape, jnp.float32),
        in_specs=[in_vmem, in_vmem, in_vmem, in_place],
        out_specs=in_place,
        input_output_aliases={3: 0},
        scratch_shapes=[
            pltpu.VMEM(partial.shape, jnp.float32),
            pltpu.SemaphoreType.DMA,
        ],
        compiler_params=pltpu.CompilerParams(vmem_limit_bytes=12 << 20),
        name="last",
    )(elim, partial, arrived, total)


def local(design, arc_partials, arc_id, arc_weight):
    row_count, col_count = lax.axis_size("row"), lax.axis_size("col")
    held, elim, ready, piece = gather(design, arc_partials, arc_id, arc_weight, row_count, col_count)
    pairs = [(1, 0), (0, 1), (col_count - 2, col_count - 1), (col_count - 1, col_count - 2)]
    arrived = lax.ppermute(piece, "col", pairs)
    total, partial = finish(held, elim, ready)
    return last(elim, partial, arrived, total, design.shape[0])


def solution(mesh):
    placed = (P(("row", "col"), None), P(("row", "col"), None, None), P(("row", "col")), P())
    return jax.shard_map(
        local, mesh=mesh, in_specs=placed, out_specs=P("row", "col"), check_vma=False
    )
```

```python
import functools

import jax
import jax.numpy as jnp
from jax import lax
from jax.experimental import pallas as pl
from jax.experimental.pallas import tpu as pltpu
from jax.sharding import PartitionSpec as P

SLAB = 2048
LANES = 128
GROUP = 8
RIDGE = 4.0
SKEW = 1
AHEAD = 3
FACTS_STEP = 3
SOLVE_AFTER = 3
LEFT = 2

MESH = pl.DeviceIdType.MESH
HIGH = lax.Precision.HIGHEST


def chunk_width(rows):
    blocks = rows // LANES
    return LANES * max(k for k in range(1, 9) if blocks % k == 0)


def narrow_width(width, col_count):
    return LANES * -(-(width // LANES) // (col_count - 1))


def partner(r, p, count):
    out, bit = 0, 1
    while bit < count:
        out = out + bit * lax.rem(r // bit + p // bit, 2)
        bit *= 2
    return out


def dot(a, b, dims):
    return lax.dot_general(a, b, (dims, ((), ())), precision=HIGH, preferred_element_type=jnp.float32)


def eliminate(facts, values, order, arcs, rows_dev):
    wide = -(-arcs * GROUP // LANES) * LANES
    lane_in = lax.broadcasted_iota(jnp.int32, (LANES, wide), 0)
    lane_out = lax.broadcasted_iota(jnp.int32, (LANES, wide), 1)
    repeat = (lane_in // rows_dev == lane_out % GROUP).astype(jnp.float32)
    epoch = lax.broadcasted_iota(jnp.int32, facts.shape, 0)
    lane = lax.broadcasted_iota(jnp.int32, facts.shape, 1)
    own = (lane % rows_dev == epoch % rows_dev) & (lane < order * rows_dev)
    partials = dot(jnp.where(own, facts, 0.0), repeat, ((1,), (0,)))
    arc = (lax.broadcasted_iota(jnp.int32, partials.shape, 1) // GROUP).astype(jnp.float32)
    at_id = order * rows_dev
    spread = jnp.where(facts[:, at_id : at_id + 1] == arc, partials, 0.0)
    rhs = dot(spread, values, ((0,), (0,))).reshape(wide // GROUP, GROUP, -1)
    gram = dot(spread, partials[:, 0:LANES], ((0,), (0,))).reshape(wide // GROUP, GROUP, LANES)
    at = lax.broadcasted_iota(jnp.int32, gram.shape, 1)
    gram = gram + jnp.where(at == lax.broadcasted_iota(jnp.int32, gram.shape, 2), RIDGE, 0.0)
    at_rhs = lax.broadcasted_iota(jnp.int32, rhs.shape, 1)
    for pivot in range(order):
        scale = 1.0 / gram[:, pivot : pivot + 1, pivot : pivot + 1]
        row_gram = gram[:, pivot : pivot + 1, :] * scale
        row_rhs = rhs[:, pivot : pivot + 1, :] * scale
        factor = gram[:, :, pivot : pivot + 1]
        gram = jnp.where(at == pivot, row_gram, gram - factor * row_gram)
        rhs = jnp.where(at_rhs == pivot, row_rhs, rhs - factor * row_rhs)
    fitted = dot(spread, rhs.reshape(wide, -1), ((1,), (0,)))
    return (facts[:, at_id + 1 : at_id + 2] * (values - fitted)).astype(jnp.bfloat16)


def product_tile(held, elim, start, tile):
    epochs = elim.shape[0] * elim.shape[1]
    return (1.0 / epochs) * lax.dot_general(
        held[:, :, pl.ds(pl.multiple_of(start, LANES), tile)].reshape(epochs, tile),
        elim[...].reshape(epochs, -1),
        (((0,), (0,)), ((), ())),
        preferred_element_type=jnp.float32,
    )


def gather_kernel(
    row_count, col_count, width,
    design, partials_in, ids, weights_in,
    held, elim, ready, piece,
    slab, facts, spread_facts, partials, weights,
    recv_z, own_down, own_up, send_down, send_up, recv_in, send_in, own_sem,
    slab_sem, facts_sem,
):
    r, c = lax.axis_index("row"), lax.axis_index("col")
    rows_dev, coefficients = design.shape
    rows = coefficients // row_count
    block = row_count * rows_dev
    columns = slab.shape[2]
    order, arcs = partials.shape[0], weights.shape[0]
    chunks = rows // width
    slab_chunks = -(-columns * col_count // width)
    peers = [partner(r, p, row_count) for p in range(row_count)]

    barrier = pltpu.get_barrier_semaphore()
    for p in range(1, row_count):
        pl.semaphore_signal(barrier, inc=1, device_id=(peers[p], c), device_id_type=MESH)
    for k in range(1, col_count):
        pl.semaphore_signal(barrier, inc=1, device_id=(r, lax.rem(c + k, col_count)), device_id_type=MESH)
    pl.semaphore_wait(barrier, row_count + col_count - 2)

    def remote(src, dst, send, recv, device):
        return pltpu.make_async_remote_copy(
            src_ref=src, dst_ref=dst, send_sem=send, recv_sem=recv, device_id=device, device_id_type=MESH
        )

    def arrived(ref, sem):
        pltpu.make_async_copy(ref, ref, sem).wait()

    def own_block(z):
        return held.at[z, pl.ds(0, rows_dev), :]

    def part(j):
        return pl.ds(pl.multiple_of(j * width, width), width)

    def chunk(z, j):
        return held.at[z, pl.ds(rows_dev, block - rows_dev), part(j)]

    narrow = narrow_width(width, col_count)
    others = pl.ds(rows_dev, block - rows_dev)

    def early(z):
        return held.at[z, others, pl.ds(rows - width, width - narrow)]

    def forward(z, unit, sems, target, last_hop, k):
        cut = last_hop & (unit == chunks)

        @pl.when(jnp.logical_not(cut))
        def _():
            ref = chunk(z, unit - 1)
            remote(ref, ref, sems.at[z], recv_z.at[z, unit], target).start()

        @pl.when(cut)
        def _():
            remote(early(z), early(z), sems.at[z], recv_z.at[z, unit], target).start()
            late = held.at[z, others, pl.ds(rows - narrow, narrow)]
            pltpu.make_async_copy(late, piece.at[k], own_sem.at[3]).start()

    before_low, before_high = c == 1, c == col_count - 2
    mine = design.at[:, pl.ds(pl.multiple_of(r * rows, LANES), rows)]
    down, up = (r, lax.max(c - 1, 0)), (r, lax.min(c + 1, col_count - 1))

    @pl.when(c > 0)
    def _():
        remote(mine, own_block(c), own_down.at[c], recv_z.at[c, 0], down).start()

    @pl.when(c < col_count - 1)
    def _():
        remote(mine, own_block(c), own_up.at[c], recv_z.at[c, 0], up).start()

    def send_chunk(j):
        for p in range(1, row_count):
            start = pl.multiple_of(peers[p] * rows + j * width, LANES)
            remote(
                design.at[:, pl.ds(start, width)],
                held.at[c, pl.ds(p * rows_dev, rows_dev), part(j)],
                send_in.at[0],
                recv_in.at[j],
                (peers[p], c),
            ).start()

    small = [
        pltpu.make_async_copy(src, dst, own_sem.at[1 + i])
        for i, (src, dst) in enumerate(((partials_in, partials), (weights_in, weights)))
    ]
    for copy in small:
        copy.start()
    for j in range(min(AHEAD, chunks)):
        send_chunk(j)
    own_copy = pltpu.make_async_copy(mine, own_block(c), own_sem.at[0])
    own_copy.start()

    for copy in small:
        copy.wait()
    lane = lax.broadcasted_iota(jnp.int32, (1, LANES), 1)
    row = jnp.where(lane == order * rows_dev, ids[0].astype(jnp.float32), 0.0)
    row = jnp.where(lane == order * rows_dev + 1, weights[ids[0]], row)
    shift_in = lax.broadcasted_iota(jnp.int32, (rows_dev, LANES), 0)
    shift_out = lax.broadcasted_iota(jnp.int32, (rows_dev, LANES), 1)
    for p in range(order):
        place = (shift_out == shift_in + p * rows_dev).astype(jnp.float32)
        row = row + dot(partials[p], place, ((1,), (0,)))
    facts[c, r] = row
    mine_facts = facts.at[c, r]
    for k in range(1, col_count):
        other = lax.rem(c + k, col_count)
        remote(mine_facts, mine_facts, facts_sem.at[0], facts_sem.at[1], (r, other)).start()
    other_facts = facts.at[pl.ds(0, col_count - 1), 0]
    rest = facts.at[:, pl.ds(0, row_count - 1)]

    def step(t, _):
        @pl.when((t + AHEAD - 1 < chunks) & (t >= 1))
        def _():
            send_chunk(t + AHEAD - 1)

        @pl.when((t >= 1) & (t <= chunks))
        def _():
            own = chunk(c, t - 1)
            arrived(own, recv_in.at[t - 1])

            @pl.when(c > 0)
            def _():
                forward(c, t, send_down, down, before_low, c - 1)

            @pl.when(c < col_count - 1)
            def _():
                forward(c, t, send_up, up, before_high, c)

        for d in range(1, col_count):
            unit = t - d * SKEW
            for z, k, exists, onward, last_hop, own_sems, sems, target in (
                (c + d, c + d - 1, c + d < col_count, c > 0, before_low, own_down, send_down, down),
                (c - d, c - d, c - d >= 0, c < col_count - 1, before_high, own_up, send_up, up),
            ):

                @pl.when((unit == 0) & exists)
                def _():
                    ref = own_block(z)
                    arrived(ref, recv_z.at[z, 0])

                    @pl.when(onward)
                    def _():
                        remote(ref, ref, own_sems.at[z], recv_z.at[z, 0], target).start()

                @pl.when((unit >= 1) & exists & ((unit < chunks) | (onward & (unit == chunks))))
                def _():
                    arrived(chunk(z, unit - 1), recv_z.at[z, unit])

                    @pl.when(onward)
                    def _():
                        forward(z, unit, sems, target, last_hop, k)

                @pl.when((unit == chunks) & exists & jnp.logical_not(onward))
                def _():
                    arrived(early(z), recv_z.at[z, unit])

        @pl.when(t == FACTS_STEP)
        def _():
            arrived(other_facts, facts_sem.at[1])
            for p in range(1, row_count):
                ref = facts.at[:, r]
                remote(ref, ref, facts_sem.at[2], facts_sem.at[3], (peers[p], c)).start()

        @pl.when((t == slab_step) & (r == 0))
        def _():
            own_copy.wait()
            source = held.at[:, :, pl.ds(pl.multiple_of(c * columns, columns), columns)]
            for p in range(1, row_count):
                remote(source, slab, slab_sem.at[0], slab_sem.at[1], (p, c)).start()
            local_slab = pltpu.make_async_copy(source, slab, slab_sem.at[2])
            local_slab.start()
            local_slab.wait()

        @pl.when(t == solve_step)
        def _():
            @pl.when(r > 0)
            def _():
                own_copy.wait()
                arrived(slab, slab_sem.at[1])

            arrived(rest, facts_sem.at[3])
            for z in range(col_count):
                for k in range(row_count):
                    spread_facts[pl.ds((z * row_count + k) * rows_dev, rows_dev), :] = jnp.broadcast_to(
                        facts[z, k], (rows_dev, LANES)
                    )
            out = eliminate(
                spread_facts[...],
                slab[...].reshape(col_count * block, columns).astype(jnp.float32),
                order,
                arcs,
                rows_dev,
            ).reshape(col_count, block, columns)
            for edge, first in ((0, 1), (col_count - 1, 0)):

                @pl.when(c == edge)
                def _():
                    piece[...] = jnp.zeros_like(piece)
                    for z in range(first, first + col_count - 1):
                        held[z, rows_dev:block, rows - narrow : rows] = jnp.zeros(
                            (block - rows_dev, narrow), jnp.bfloat16
                        )

            for k in range(row_count):
                at = pl.ds(pl.multiple_of(peers[k] * rows_dev, rows_dev), rows_dev)
                elim[:, at, :] = out[:, k * rows_dev : (k + 1) * rows_dev, :]

        here = lax.min(lax.max(t - (col_count - 1) * SKEW, 0), chunks - LEFT)
        before = lax.min(lax.max(t - 1 - (col_count - 1) * SKEW, 0), chunks - LEFT)

        @pl.when(t >= solve_step)
        def _():
            def form(j, _):
                ready[part(j), :] = product_tile(held, elim, j * width, width)
                return 0

            lax.fori_loop(lax.select(t == solve_step, 0, before), here, form, 0)

        return 0

    slab_step = slab_chunks + (col_count - 1) * SKEW
    solve_step = slab_step + SOLVE_AFTER
    lax.fori_loop(0, chunks + 1 + (col_count - 1) * SKEW, step, 0)

    sent = design.at[:, pl.ds(0, (row_count - 1) * rows)]
    arrived(sent, send_in.at[0])
    arrived(other_facts, facts_sem.at[0])
    arrived(rest, facts_sem.at[2])

    @pl.when(r == 0)
    def _():
        share = held.at[:, :, pl.ds(0, (row_count - 1) * columns)]
        arrived(share, slab_sem.at[0])

    for z in range(col_count):
        for sends, last_hop, own_sems, sems in (
            ((c > 0) & (z >= c), before_low, own_down, send_down),
            ((c < col_count - 1) & (z <= c), before_high, own_up, send_up),
        ):

            @pl.when(sends)
            def _():
                arrived(own_block(z), own_sems.at[z])

            @pl.when(sends & last_hop)
            def _():
                arrived(held.at[z, others, pl.ds(0, rows - narrow)], sems.at[z])

            @pl.when(sends & jnp.logical_not(last_hop))
            def _():
                arrived(held.at[z, others, :], sems.at[z])

    @pl.when(before_low | before_high)
    def _():
        arrived(piece, own_sem.at[3])


def in_hbm(array):
    return pltpu.with_memory_space_constraint(array, pltpu.HBM)


def gather(design, arc_partials, arc_id, arc_weight, row_count, col_count):
    rows_dev, coefficients = design.shape
    rows = coefficients // row_count
    columns = SLAB // col_count
    block = rows_dev * row_count
    width = chunk_width(rows)
    chunks = rows // width
    dma = pltpu.SemaphoreType.DMA
    partials = arc_partials.transpose(1, 0, 2)
    in_vmem = pl.BlockSpec(memory_space=pltpu.VMEM)
    return pl.pallas_call(
        functools.partial(gather_kernel, row_count, col_count, width),
        out_shape=(
            pltpu.VMEM((col_count, block, rows), jnp.bfloat16),
            pltpu.VMEM((col_count, block, columns), jnp.bfloat16),
            pltpu.VMEM((rows - LEFT * width, columns), jnp.float32),
            pltpu.VMEM((col_count - 1, block - rows_dev, narrow_width(width, col_count)), jnp.bfloat16),
        ),
        in_specs=[
            pl.BlockSpec(memory_space=pltpu.HBM),
            pl.BlockSpec(memory_space=pltpu.HBM),
            pl.BlockSpec(memory_space=pltpu.SMEM),
            pl.BlockSpec(memory_space=pltpu.HBM),
        ],
        out_specs=(in_vmem,) * 4,
        scratch_shapes=[
            pltpu.VMEM((col_count, block, columns), jnp.bfloat16),
            pltpu.VMEM((col_count, row_count, 1, LANES), jnp.float32),
            pltpu.VMEM((col_count * block, LANES), jnp.float32),
            pltpu.VMEM(partials.shape, jnp.float32),
            pltpu.SMEM(arc_weight.shape, jnp.float32),
            dma((col_count, chunks + 1)),
            dma((col_count,)),
            dma((col_count,)),
            dma((col_count,)),
            dma((col_count,)),
            dma((chunks,)),
            dma((1,)),
            dma((4,)),
            dma((3,)),
            dma((4,)),
        ],
        compiler_params=pltpu.CompilerParams(
            collective_id=0, has_side_effects=True, vmem_limit_bytes=16 << 20
        ),
        name="gather",
    )(in_hbm(design), in_hbm(partials), arc_id, in_hbm(arc_weight))


def finish_kernel(size, held, elim, ready, out, partial, tile, sems):
    rows = out.shape[0]
    count = ready.shape[0] // size
    narrow = partial.shape[0]
    copies = [
        pltpu.make_async_copy(ready.at[at, :], out.at[at, :], sems.at[i])
        for i, at in enumerate(pl.ds(i * size, size) for i in range(count))
    ]
    for copy in copies:
        copy.start()
    for k, (start, length) in enumerate(((rows - LEFT * size, size), (rows - size, size - narrow))):
        tile[k, 0:length, :] = product_tile(held, elim, start, length)
        to = out.at[pl.ds(start, length), :]
        copies.append(pltpu.make_async_copy(tile.at[k, pl.ds(0, length), :], to, sems.at[count + k]))
        copies[-1].start()
    partial[...] = product_tile(held, elim, rows - narrow, narrow)
    for copy in copies:
        copy.wait()


def finish(held, elim, ready):
    col_count, block, rows = held.shape
    columns = elim.shape[2]
    width = chunk_width(rows)
    in_vmem = pl.BlockSpec(memory_space=pltpu.VMEM)
    return pl.pallas_call(
        functools.partial(finish_kernel, width),
        out_shape=(
            jax.ShapeDtypeStruct((rows, columns), jnp.float32),
            pltpu.VMEM((narrow_width(width, col_count), columns), jnp.float32),
        ),
        in_specs=[in_vmem, in_vmem, in_vmem],
        out_specs=(pl.BlockSpec(memory_space=pl.ANY), in_vmem),
        scratch_shapes=[
            pltpu.VMEM((LEFT, width, columns), jnp.float32),
            pltpu.SemaphoreType.DMA((rows // width,)),
        ],
        compiler_params=pltpu.CompilerParams(vmem_limit_bytes=12 << 20),
        cost_estimate=pl.CostEstimate(
            flops=2 * LEFT * col_count * block * width * columns,
            bytes_accessed=4 * rows * columns,
            transcendentals=0,
        ),
        name="finish",
    )(held, elim, ready)


def last_kernel(scale, rows_dev, elim, partial, arrived, total, out, tile, sem):
    col_count, block, _ = elim.shape
    narrow = partial.shape[0]
    first = lax.select(lax.axis_index("col") == 0, 1, 0)
    late = elim[pl.ds(first, col_count - 1), rows_dev:block, :].reshape(-1, tile.shape[1])
    rows = arrived[...].reshape(late.shape[0], narrow)
    tile[...] = partial[...] + scale * lax.dot_general(
        rows, late, (((0,), (0,)), ((), ())), preferred_element_type=jnp.float32
    )
    copy = pltpu.make_async_copy(tile, out.at[pl.ds(out.shape[0] - narrow, narrow), :], sem)
    copy.start()
    copy.wait()


def last(elim, partial, arrived, total, rows_dev):
    col_count, block, columns = elim.shape
    in_vmem = pl.BlockSpec(memory_space=pltpu.VMEM)
    in_place = pl.BlockSpec(memory_space=pl.ANY)
    return pl.pallas_call(
        functools.partial(last_kernel, 1.0 / (col_count * block), rows_dev),
        out_shape=jax.ShapeDtypeStruct(total.shape, jnp.float32),
        in_specs=[in_vmem, in_vmem, in_vmem, in_place],
        out_specs=in_place,
        input_output_aliases={3: 0},
        scratch_shapes=[
            pltpu.VMEM(partial.shape, jnp.float32),
            pltpu.SemaphoreType.DMA,
        ],
        compiler_params=pltpu.CompilerParams(vmem_limit_bytes=12 << 20),
        name="last",
    )(elim, partial, arrived, total)


def local(design, arc_partials, arc_id, arc_weight):
    row_count, col_count = lax.axis_size("row"), lax.axis_size("col")
    held, elim, ready, piece = gather(design, arc_partials, arc_id, arc_weight, row_count, col_count)
    pairs = [(1, 0), (0, 1), (col_count - 2, col_count - 1), (col_count - 1, col_count - 2)]
    arrived = lax.ppermute(piece, "col", pairs)
    total, partial = finish(held, elim, ready)
    return last(elim, partial, arrived, total, design.shape[0])


def solution(mesh):
    placed = (P(("row", "col"), None), P(("row", "col"), None, None), P(("row", "col")), P())
    return jax.shard_map(
        local, mesh=mesh, in_specs=placed, out_specs=P("row", "col"), check_vma=False
    )
```

```python
import functools

import jax
import jax.numpy as jnp
from jax import lax
from jax.experimental import pallas as pl
from jax.experimental.pallas import tpu as pltpu
from jax.sharding import PartitionSpec as P

SLAB = 2048
LANES = 128
GROUP = 8
RIDGE = 4.0
SKEW = 1
AHEAD = 3
FACTS_STEP = 3
SOLVE_AFTER = 3
LEFT = 2

MESH = pl.DeviceIdType.MESH
HIGH = lax.Precision.HIGHEST


def chunk_width(rows):
    blocks = rows // LANES
    return LANES * max(k for k in range(1, 9) if blocks % k == 0)


def narrow_width(width, col_count):
    return LANES * -(-(width // LANES) // (col_count - 1))


def partners(r, count):
    out, bit = [r], 1
    while bit < count:
        step = bit * (1 - 2 * lax.rem(lax.div(r, bit), 2))
        out = out + [row + step for row in out]
        bit *= 2
    return out


def dot(a, b, dims):
    return lax.dot_general(a, b, (dims, ((), ())), precision=HIGH, preferred_element_type=jnp.float32)


def eliminate(facts, values, order, arcs, rows_dev):
    wide = -(-arcs * GROUP // LANES) * LANES
    lane_in = lax.broadcasted_iota(jnp.int32, (LANES, wide), 0)
    lane_out = lax.broadcasted_iota(jnp.int32, (LANES, wide), 1)
    repeat = (lane_in // rows_dev == lane_out % GROUP).astype(jnp.float32)
    epoch = lax.broadcasted_iota(jnp.int32, facts.shape, 0)
    lane = lax.broadcasted_iota(jnp.int32, facts.shape, 1)
    own = (lane % rows_dev == epoch % rows_dev) & (lane < order * rows_dev)
    partials = dot(jnp.where(own, facts, 0.0), repeat, ((1,), (0,)))
    arc = (lax.broadcasted_iota(jnp.int32, partials.shape, 1) // GROUP).astype(jnp.float32)
    at_id = order * rows_dev
    spread = jnp.where(facts[:, at_id : at_id + 1] == arc, partials, 0.0)
    rhs = dot(spread, values, ((0,), (0,))).reshape(wide // GROUP, GROUP, -1)
    gram = dot(spread, partials[:, 0:LANES], ((0,), (0,))).reshape(wide // GROUP, GROUP, LANES)
    at = lax.broadcasted_iota(jnp.int32, gram.shape, 1)
    gram = gram + jnp.where(at == lax.broadcasted_iota(jnp.int32, gram.shape, 2), RIDGE, 0.0)
    at_rhs = lax.broadcasted_iota(jnp.int32, rhs.shape, 1)
    for pivot in range(order):
        scale = 1.0 / gram[:, pivot : pivot + 1, pivot : pivot + 1]
        row_gram = gram[:, pivot : pivot + 1, :] * scale
        row_rhs = rhs[:, pivot : pivot + 1, :] * scale
        factor = gram[:, :, pivot : pivot + 1]
        gram = jnp.where(at == pivot, row_gram, gram - factor * row_gram)
        rhs = jnp.where(at_rhs == pivot, row_rhs, rhs - factor * row_rhs)
    fitted = dot(spread, rhs.reshape(wide, -1), ((1,), (0,)))
    return (facts[:, at_id + 1 : at_id + 2] * (values - fitted)).astype(jnp.bfloat16)


def product_tile(held, elim, start, tile):
    epochs = elim.shape[0] * elim.shape[1]
    return (1.0 / epochs) * lax.dot_general(
        held[:, :, pl.ds(pl.multiple_of(start, LANES), tile)].reshape(epochs, tile),
        elim[...].reshape(epochs, -1),
        (((0,), (0,)), ((), ())),
        preferred_element_type=jnp.float32,
    )


def gather_kernel(
    row_count, col_count, width,
    design, partials_in, ids, weights_in,
    held, elim, ready, piece,
    slab, facts, spread_facts, partials, weights,
    recv_z, own_down, own_up, send_down, send_up, recv_in, send_in, own_sem,
    slab_sem, facts_sem,
):
    r, c = lax.axis_index("row"), lax.axis_index("col")
    rows_dev, coefficients = design.shape
    rows = coefficients // row_count
    block = row_count * rows_dev
    columns = slab.shape[2]
    order, arcs = partials.shape[0], weights.shape[0]
    chunks = rows // width
    slab_chunks = -(-columns * col_count // width)
    peers = partners(r, row_count)

    barrier = pltpu.get_barrier_semaphore()
    for p in range(1, row_count):
        pl.semaphore_signal(barrier, inc=1, device_id=(peers[p], c), device_id_type=MESH)
    for k in range(1, col_count):
        pl.semaphore_signal(barrier, inc=1, device_id=(r, lax.rem(c + k, col_count)), device_id_type=MESH)
    pl.semaphore_wait(barrier, row_count + col_count - 2)

    def remote(src, dst, send, recv, device):
        return pltpu.make_async_remote_copy(
            src_ref=src, dst_ref=dst, send_sem=send, recv_sem=recv, device_id=device, device_id_type=MESH
        )

    def arrived(ref, sem):
        pltpu.make_async_copy(ref, ref, sem).wait()

    def own_block(z):
        return held.at[z, pl.ds(0, rows_dev), :]

    def part(j):
        return pl.ds(pl.multiple_of(j * width, width), width)

    def chunk(z, j):
        return held.at[z, pl.ds(rows_dev, block - rows_dev), part(j)]

    narrow = narrow_width(width, col_count)
    others = pl.ds(rows_dev, block - rows_dev)

    def early(z):
        return held.at[z, others, pl.ds(rows - width, width - narrow)]

    def forward(z, unit, sems, target, last_hop, k):
        cut = last_hop & (unit == chunks)

        @pl.when(jnp.logical_not(cut))
        def _():
            ref = chunk(z, unit - 1)
            remote(ref, ref, sems.at[z], recv_z.at[z, unit], target).start()

        @pl.when(cut)
        def _():
            remote(early(z), early(z), sems.at[z], recv_z.at[z, unit], target).start()
            late = held.at[z, others, pl.ds(rows - narrow, narrow)]
            pltpu.make_async_copy(late, piece.at[k], own_sem.at[3]).start()

    before_low, before_high = c == 1, c == col_count - 2
    mine = design.at[:, pl.ds(pl.multiple_of(r * rows, LANES), rows)]
    down, up = (r, lax.max(c - 1, 0)), (r, lax.min(c + 1, col_count - 1))

    @pl.when(c > 0)
    def _():
        remote(mine, own_block(c), own_down.at[c], recv_z.at[c, 0], down).start()

    @pl.when(c < col_count - 1)
    def _():
        remote(mine, own_block(c), own_up.at[c], recv_z.at[c, 0], up).start()

    def send_chunk(j):
        for p in range(1, row_count):
            start = pl.multiple_of(peers[p] * rows + j * width, LANES)
            remote(
                design.at[:, pl.ds(start, width)],
                held.at[c, pl.ds(p * rows_dev, rows_dev), part(j)],
                send_in.at[0],
                recv_in.at[j],
                (peers[p], c),
            ).start()

    small = [
        pltpu.make_async_copy(src, dst, own_sem.at[1 + i])
        for i, (src, dst) in enumerate(((partials_in, partials), (weights_in, weights)))
    ]
    for copy in small:
        copy.start()
    for j in range(min(AHEAD, chunks)):
        send_chunk(j)
    own_copy = pltpu.make_async_copy(mine, own_block(c), own_sem.at[0])
    own_copy.start()

    for copy in small:
        copy.wait()
    lane = lax.broadcasted_iota(jnp.int32, (1, LANES), 1)
    row = jnp.where(lane == order * rows_dev, ids[0].astype(jnp.float32), 0.0)
    row = jnp.where(lane == order * rows_dev + 1, weights[ids[0]], row)
    shift_in = lax.broadcasted_iota(jnp.int32, (rows_dev, LANES), 0)
    shift_out = lax.broadcasted_iota(jnp.int32, (rows_dev, LANES), 1)
    for p in range(order):
        place = (shift_out == shift_in + p * rows_dev).astype(jnp.float32)
        row = row + dot(partials[p], place, ((1,), (0,)))
    facts[c, r] = row
    mine_facts = facts.at[c, r]
    for k in range(1, col_count):
        other = lax.rem(c + k, col_count)
        remote(mine_facts, mine_facts, facts_sem.at[0], facts_sem.at[1], (r, other)).start()
    other_facts = facts.at[pl.ds(0, col_count - 1), 0]
    rest = facts.at[:, pl.ds(0, row_count - 1)]

    def step(t, _):
        @pl.when((t + AHEAD - 1 < chunks) & (t >= 1))
        def _():
            send_chunk(t + AHEAD - 1)

        @pl.when((t >= 1) & (t <= chunks))
        def _():
            own = chunk(c, t - 1)
            arrived(own, recv_in.at[t - 1])

            @pl.when(c > 0)
            def _():
                forward(c, t, send_down, down, before_low, c - 1)

            @pl.when(c < col_count - 1)
            def _():
                forward(c, t, send_up, up, before_high, c)

        for d in range(1, col_count):
            unit = t - d * SKEW
            for z, k, exists, onward, last_hop, own_sems, sems, target in (
                (c + d, c + d - 1, c + d < col_count, c > 0, before_low, own_down, send_down, down),
                (c - d, c - d, c - d >= 0, c < col_count - 1, before_high, own_up, send_up, up),
            ):

                @pl.when((unit == 0) & exists)
                def _():
                    ref = own_block(z)
                    arrived(ref, recv_z.at[z, 0])

                    @pl.when(onward)
                    def _():
                        remote(ref, ref, own_sems.at[z], recv_z.at[z, 0], target).start()

                @pl.when((unit >= 1) & exists & ((unit < chunks) | (onward & (unit == chunks))))
                def _():
                    arrived(chunk(z, unit - 1), recv_z.at[z, unit])

                    @pl.when(onward)
                    def _():
                        forward(z, unit, sems, target, last_hop, k)

                @pl.when((unit == chunks) & exists & jnp.logical_not(onward))
                def _():
                    arrived(early(z), recv_z.at[z, unit])

        @pl.when(t == FACTS_STEP)
        def _():
            arrived(other_facts, facts_sem.at[1])
            for p in range(1, row_count):
                ref = facts.at[:, r]
                remote(ref, ref, facts_sem.at[2], facts_sem.at[3], (peers[p], c)).start()

        @pl.when((t == slab_step) & (r == 0))
        def _():
            own_copy.wait()
            source = held.at[:, :, pl.ds(pl.multiple_of(c * columns, columns), columns)]
            for p in range(1, row_count):
                remote(source, slab, slab_sem.at[0], slab_sem.at[1], (p, c)).start()
            local_slab = pltpu.make_async_copy(source, slab, slab_sem.at[2])
            local_slab.start()
            local_slab.wait()

        @pl.when(t == solve_step)
        def _():
            @pl.when(r > 0)
            def _():
                own_copy.wait()
                arrived(slab, slab_sem.at[1])

            arrived(rest, facts_sem.at[3])
            for z in range(col_count):
                for k in range(row_count):
                    spread_facts[pl.ds((z * row_count + k) * rows_dev, rows_dev), :] = jnp.broadcast_to(
                        facts[z, k], (rows_dev, LANES)
                    )
            out = eliminate(
                spread_facts[...],
                slab[...].reshape(col_count * block, columns).astype(jnp.float32),
                order,
                arcs,
                rows_dev,
            ).reshape(col_count, block, columns)
            for edge, first in ((0, 1), (col_count - 1, 0)):

                @pl.when(c == edge)
                def _():
                    piece[...] = jnp.zeros_like(piece)
                    for z in range(first, first + col_count - 1):
                        held[z, rows_dev:block, rows - narrow : rows] = jnp.zeros(
                            (block - rows_dev, narrow), jnp.bfloat16
                        )

            for k in range(row_count):
                at = pl.ds(pl.multiple_of(peers[k] * rows_dev, rows_dev), rows_dev)
                elim[:, at, :] = out[:, k * rows_dev : (k + 1) * rows_dev, :]

        @pl.when(t == chunks + 1)
        def _():
            sent = design.at[:, pl.ds(0, (row_count - 1) * rows)]
            arrived(sent, send_in.at[0])
            arrived(other_facts, facts_sem.at[0])
            arrived(rest, facts_sem.at[2])

            @pl.when(r == 0)
            def _():
                share = held.at[:, :, pl.ds(0, (row_count - 1) * columns)]
                arrived(share, slab_sem.at[0])

        here = lax.min(lax.max(t - (col_count - 1) * SKEW, 0), chunks - LEFT)
        before = lax.min(lax.max(t - 1 - (col_count - 1) * SKEW, 0), chunks - LEFT)

        @pl.when(t >= solve_step)
        def _():
            def form(j, _):
                ready[part(j), :] = product_tile(held, elim, j * width, width)
                return 0

            lax.fori_loop(lax.select(t == solve_step, 0, before), here, form, 0)

        return 0

    slab_step = slab_chunks + (col_count - 1) * SKEW
    solve_step = slab_step + SOLVE_AFTER
    lax.fori_loop(0, chunks + 1 + (col_count - 1) * SKEW, step, 0)

    for z in range(col_count):
        for sends, last_hop, own_sems, sems in (
            ((c > 0) & (z >= c), before_low, own_down, send_down),
            ((c < col_count - 1) & (z <= c), before_high, own_up, send_up),
        ):

            @pl.when(sends)
            def _():
                arrived(own_block(z), own_sems.at[z])

            @pl.when(sends & last_hop)
            def _():
                arrived(held.at[z, others, pl.ds(0, rows - narrow)], sems.at[z])

            @pl.when(sends & jnp.logical_not(last_hop))
            def _():
                arrived(held.at[z, others, :], sems.at[z])

    @pl.when(before_low | before_high)
    def _():
        arrived(piece, own_sem.at[3])


def in_hbm(array):
    return pltpu.with_memory_space_constraint(array, pltpu.HBM)


def gather(design, arc_partials, arc_id, arc_weight, row_count, col_count):
    rows_dev, coefficients = design.shape
    rows = coefficients // row_count
    columns = SLAB // col_count
    block = rows_dev * row_count
    width = chunk_width(rows)
    chunks = rows // width
    dma = pltpu.SemaphoreType.DMA
    partials = arc_partials.transpose(1, 0, 2)
    in_vmem = pl.BlockSpec(memory_space=pltpu.VMEM)
    return pl.pallas_call(
        functools.partial(gather_kernel, row_count, col_count, width),
        out_shape=(
            pltpu.VMEM((col_count, block, rows), jnp.bfloat16),
            pltpu.VMEM((col_count, block, columns), jnp.bfloat16),
            pltpu.VMEM((rows - LEFT * width, columns), jnp.float32),
            pltpu.VMEM((col_count - 1, block - rows_dev, narrow_width(width, col_count)), jnp.bfloat16),
        ),
        in_specs=[
            pl.BlockSpec(memory_space=pltpu.HBM),
            pl.BlockSpec(memory_space=pltpu.HBM),
            pl.BlockSpec(memory_space=pltpu.SMEM),
            pl.BlockSpec(memory_space=pltpu.HBM),
        ],
        out_specs=(in_vmem,) * 4,
        scratch_shapes=[
            pltpu.VMEM((col_count, block, columns), jnp.bfloat16),
            pltpu.VMEM((col_count, row_count, 1, LANES), jnp.float32),
            pltpu.VMEM((col_count * block, LANES), jnp.float32),
            pltpu.VMEM(partials.shape, jnp.float32),
            pltpu.SMEM(arc_weight.shape, jnp.float32),
            dma((col_count, chunks + 1)),
            dma((col_count,)),
            dma((col_count,)),
            dma((col_count,)),
            dma((col_count,)),
            dma((chunks,)),
            dma((1,)),
            dma((4,)),
            dma((3,)),
            dma((4,)),
        ],
        compiler_params=pltpu.CompilerParams(
            collective_id=0, has_side_effects=True, vmem_limit_bytes=16 << 20
        ),
        name="gather",
    )(in_hbm(design), in_hbm(partials), arc_id, in_hbm(arc_weight))


def finish_kernel(size, held, elim, ready, out, partial, tile, sems):
    rows = out.shape[0]
    count = ready.shape[0] // size
    narrow = partial.shape[0]
    copies = [
        pltpu.make_async_copy(ready.at[at, :], out.at[at, :], sems.at[i])
        for i, at in enumerate(pl.ds(i * size, size) for i in range(count))
    ]
    for copy in copies:
        copy.start()
    for k, (start, length) in enumerate(((rows - LEFT * size, size), (rows - size, size - narrow))):
        tile[k, 0:length, :] = product_tile(held, elim, start, length)
        to = out.at[pl.ds(start, length), :]
        copies.append(pltpu.make_async_copy(tile.at[k, pl.ds(0, length), :], to, sems.at[count + k]))
        copies[-1].start()
    partial[...] = product_tile(held, elim, rows - narrow, narrow)
    for copy in copies:
        copy.wait()


def finish(held, elim, ready):
    col_count, block, rows = held.shape
    columns = elim.shape[2]
    width = chunk_width(rows)
    in_vmem = pl.BlockSpec(memory_space=pltpu.VMEM)
    return pl.pallas_call(
        functools.partial(finish_kernel, width),
        out_shape=(
            jax.ShapeDtypeStruct((rows, columns), jnp.float32),
            pltpu.VMEM((narrow_width(width, col_count), columns), jnp.float32),
        ),
        in_specs=[in_vmem, in_vmem, in_vmem],
        out_specs=(pl.BlockSpec(memory_space=pl.ANY), in_vmem),
        scratch_shapes=[
            pltpu.VMEM((LEFT, width, columns), jnp.float32),
            pltpu.SemaphoreType.DMA((rows // width,)),
        ],
        compiler_params=pltpu.CompilerParams(vmem_limit_bytes=12 << 20),
        cost_estimate=pl.CostEstimate(
            flops=2 * LEFT * col_count * block * width * columns,
            bytes_accessed=4 * rows * columns,
            transcendentals=0,
        ),
        name="finish",
    )(held, elim, ready)


def last_kernel(scale, rows_dev, elim, partial, arrived, total, out, tile, sem):
    col_count, block, _ = elim.shape
    narrow = partial.shape[0]
    first = lax.select(lax.axis_index("col") == 0, 1, 0)
    value = partial[...]
    for k in range(col_count - 1):
        value = value + scale * lax.dot_general(
            arrived[k],
            elim[first + k, rows_dev:block, :],
            (((0,), (0,)), ((), ())),
            preferred_element_type=jnp.float32,
        )
    tile[...] = value
    copy = pltpu.make_async_copy(tile, out.at[pl.ds(out.shape[0] - narrow, narrow), :], sem)
    copy.start()
    copy.wait()


def last(elim, partial, arrived, total, rows_dev):
    col_count, block, columns = elim.shape
    in_vmem = pl.BlockSpec(memory_space=pltpu.VMEM)
    in_place = pl.BlockSpec(memory_space=pl.ANY)
    return pl.pallas_call(
        functools.partial(last_kernel, 1.0 / (col_count * block), rows_dev),
        out_shape=jax.ShapeDtypeStruct(total.shape, jnp.float32),
        in_specs=[in_vmem, in_vmem, in_vmem, in_place],
        out_specs=in_place,
        input_output_aliases={3: 0},
        scratch_shapes=[
            pltpu.VMEM(partial.shape, jnp.float32),
            pltpu.SemaphoreType.DMA,
        ],
        compiler_params=pltpu.CompilerParams(vmem_limit_bytes=12 << 20),
        name="last",
    )(elim, partial, arrived, total)


def local(design, arc_partials, arc_id, arc_weight):
    row_count, col_count = lax.axis_size("row"), lax.axis_size("col")
    held, elim, ready, piece = gather(design, arc_partials, arc_id, arc_weight, row_count, col_count)
    pairs = [(1, 0), (0, 1), (col_count - 2, col_count - 1), (col_count - 1, col_count - 2)]
    arrived = lax.ppermute(piece, "col", pairs)
    total, partial = finish(held, elim, ready)
    return last(elim, partial, arrived, total, design.shape[0])


def solution(mesh):
    placed = (P(("row", "col"), None), P(("row", "col"), None, None), P(("row", "col")), P())
    return jax.shard_map(
        local, mesh=mesh, in_specs=placed, out_specs=P("row", "col"), check_vma=False
    )
```

```python
import functools

import jax
import jax.numpy as jnp
from jax import lax
from jax.experimental import pallas as pl
from jax.experimental.pallas import tpu as pltpu
from jax.sharding import PartitionSpec as P

SLAB = 2048
LANES = 128
GROUP = 8
RIDGE = 4.0
SKEW = 1
AHEAD = 3
FACTS_STEP = 3
SOLVE_AFTER = 3
LEFT = 2

MESH = pl.DeviceIdType.MESH
HIGH = lax.Precision.HIGHEST


def chunk_width(rows):
    blocks = rows // LANES
    return LANES * max(k for k in range(1, 9) if blocks % k == 0)


def narrow_width(width, col_count):
    return LANES * -(-(width // LANES) // (col_count - 1))


def partners(r, count):
    out, bit = [r], 1
    while bit < count:
        step = bit * (1 - 2 * lax.rem(lax.div(r, bit), 2))
        out = out + [row + step for row in out]
        bit *= 2
    return out


def dot(a, b, dims):
    return lax.dot_general(a, b, (dims, ((), ())), precision=HIGH, preferred_element_type=jnp.float32)


def eliminate(facts, values, order, arcs, rows_dev):
    wide = -(-arcs * GROUP // LANES) * LANES
    lane_in = lax.broadcasted_iota(jnp.int32, (LANES, wide), 0)
    lane_out = lax.broadcasted_iota(jnp.int32, (LANES, wide), 1)
    repeat = (lane_in // rows_dev == lane_out % GROUP).astype(jnp.float32)
    epoch = lax.broadcasted_iota(jnp.int32, facts.shape, 0)
    lane = lax.broadcasted_iota(jnp.int32, facts.shape, 1)
    own = (lane % rows_dev == epoch % rows_dev) & (lane < order * rows_dev)
    partials = dot(jnp.where(own, facts, 0.0), repeat, ((1,), (0,)))
    arc = (lax.broadcasted_iota(jnp.int32, partials.shape, 1) // GROUP).astype(jnp.float32)
    at_id = order * rows_dev
    spread = jnp.where(facts[:, at_id : at_id + 1] == arc, partials, 0.0)
    rhs = dot(spread, values, ((0,), (0,))).reshape(wide // GROUP, GROUP, -1)
    gram = dot(spread, partials[:, 0:LANES], ((0,), (0,))).reshape(wide // GROUP, GROUP, LANES)
    at = lax.broadcasted_iota(jnp.int32, gram.shape, 1)
    gram = gram + jnp.where(at == lax.broadcasted_iota(jnp.int32, gram.shape, 2), RIDGE, 0.0)
    at_rhs = lax.broadcasted_iota(jnp.int32, rhs.shape, 1)
    for pivot in range(order):
        scale = 1.0 / gram[:, pivot : pivot + 1, pivot : pivot + 1]
        row_gram = gram[:, pivot : pivot + 1, :] * scale
        row_rhs = rhs[:, pivot : pivot + 1, :] * scale
        factor = gram[:, :, pivot : pivot + 1]
        gram = jnp.where(at == pivot, row_gram, gram - factor * row_gram)
        rhs = jnp.where(at_rhs == pivot, row_rhs, rhs - factor * row_rhs)
    fitted = dot(spread, rhs.reshape(wide, -1), ((1,), (0,)))
    return (facts[:, at_id + 1 : at_id + 2] * (values - fitted)).astype(jnp.bfloat16)


def product_tile(held, elim, start, tile):
    epochs = elim.shape[0] * elim.shape[1]
    return (1.0 / epochs) * lax.dot_general(
        held[:, :, pl.ds(pl.multiple_of(start, LANES), tile)].reshape(epochs, tile),
        elim[...].reshape(epochs, -1),
        (((0,), (0,)), ((), ())),
        preferred_element_type=jnp.float32,
    )


def gather_kernel(
    row_count, col_count, width,
    design, partials_in, ids, weights_in,
    held, elim, ready, piece,
    slab, facts, spread_facts, partials, weights,
    recv_z, own_down, own_up, send_down, send_up, recv_in, send_in, own_sem,
    slab_sem, facts_sem,
):
    r, c = lax.axis_index("row"), lax.axis_index("col")
    rows_dev, coefficients = design.shape
    rows = coefficients // row_count
    block = row_count * rows_dev
    columns = slab.shape[2]
    order, arcs = partials.shape[0], weights.shape[0]
    chunks = rows // width
    slab_chunks = -(-columns * col_count // width)
    peers = partners(r, row_count)

    barrier = pltpu.get_barrier_semaphore()
    for p in range(1, row_count):
        pl.semaphore_signal(barrier, inc=1, device_id=(peers[p], c), device_id_type=MESH)
    for k in range(1, col_count):
        pl.semaphore_signal(barrier, inc=1, device_id=(r, lax.rem(c + k, col_count)), device_id_type=MESH)
    pl.semaphore_wait(barrier, row_count + col_count - 2)

    def remote(src, dst, send, recv, device):
        return pltpu.make_async_remote_copy(
            src_ref=src, dst_ref=dst, send_sem=send, recv_sem=recv, device_id=device, device_id_type=MESH
        )

    def arrived(ref, sem):
        pltpu.make_async_copy(ref, ref, sem).wait()

    def own_block(z):
        return held.at[z, pl.ds(0, rows_dev), :]

    def part(j):
        return pl.ds(pl.multiple_of(j * width, width), width)

    def chunk(z, j):
        return held.at[z, pl.ds(rows_dev, block - rows_dev), part(j)]

    narrow = narrow_width(width, col_count)
    others = pl.ds(rows_dev, block - rows_dev)

    def early(z):
        return held.at[z, others, pl.ds(rows - width, width - narrow)]

    def forward(z, unit, sems, target, last_hop, k):
        cut = last_hop & (unit == chunks)

        @pl.when(jnp.logical_not(cut))
        def _():
            ref = chunk(z, unit - 1)
            remote(ref, ref, sems.at[z], recv_z.at[z, unit], target).start()

        @pl.when(cut)
        def _():
            remote(early(z), early(z), sems.at[z], recv_z.at[z, unit], target).start()
            late = held.at[z, others, pl.ds(rows - narrow, narrow)]
            pltpu.make_async_copy(late, piece.at[k], own_sem.at[3]).start()

    before_low, before_high = c == 1, c == col_count - 2
    mine = design.at[:, pl.ds(pl.multiple_of(r * rows, LANES), rows)]
    down, up = (r, lax.max(c - 1, 0)), (r, lax.min(c + 1, col_count - 1))

    @pl.when(c > 0)
    def _():
        remote(mine, own_block(c), own_down.at[c], recv_z.at[c, 0], down).start()

    @pl.when(c < col_count - 1)
    def _():
        remote(mine, own_block(c), own_up.at[c], recv_z.at[c, 0], up).start()

    def send_chunk(j):
        for p in range(1, row_count):
            start = pl.multiple_of(peers[p] * rows + j * width, LANES)
            remote(
                design.at[:, pl.ds(start, width)],
                held.at[c, pl.ds(p * rows_dev, rows_dev), part(j)],
                send_in.at[0],
                recv_in.at[j],
                (peers[p], c),
            ).start()

    small = [
        pltpu.make_async_copy(src, dst, own_sem.at[1 + i])
        for i, (src, dst) in enumerate(((partials_in, partials), (weights_in, weights)))
    ]
    for copy in small:
        copy.start()
    for j in range(min(AHEAD, chunks)):
        send_chunk(j)
    own_copy = pltpu.make_async_copy(mine, own_block(c), own_sem.at[0])
    own_copy.start()

    for copy in small:
        copy.wait()
    lane = lax.broadcasted_iota(jnp.int32, (1, LANES), 1)
    row = jnp.where(lane == order * rows_dev, ids[0].astype(jnp.float32), 0.0)
    row = jnp.where(lane == order * rows_dev + 1, weights[ids[0]], row)
    shift_in = lax.broadcasted_iota(jnp.int32, (rows_dev, LANES), 0)
    shift_out = lax.broadcasted_iota(jnp.int32, (rows_dev, LANES), 1)
    for p in range(order):
        place = (shift_out == shift_in + p * rows_dev).astype(jnp.float32)
        row = row + dot(partials[p], place, ((1,), (0,)))
    facts[c, r] = row
    mine_facts = facts.at[c, r]
    for k in range(1, col_count):
        other = lax.rem(c + k, col_count)
        remote(mine_facts, mine_facts, facts_sem.at[0], facts_sem.at[1], (r, other)).start()
    other_facts = facts.at[pl.ds(0, col_count - 1), 0]
    rest = facts.at[:, pl.ds(0, row_count - 1)]

    def step(t, _):
        @pl.when((t + AHEAD - 1 < chunks) & (t >= 1))
        def _():
            send_chunk(t + AHEAD - 1)

        @pl.when((t >= 1) & (t <= chunks))
        def _():
            own = chunk(c, t - 1)
            arrived(own, recv_in.at[t - 1])

            @pl.when(c > 0)
            def _():
                forward(c, t, send_down, down, before_low, c - 1)

            @pl.when(c < col_count - 1)
            def _():
                forward(c, t, send_up, up, before_high, c)

        for d in range(1, col_count):
            unit = t - d * SKEW
            for z, k, exists, onward, last_hop, own_sems, sems, target in (
                (c + d, c + d - 1, c + d < col_count, c > 0, before_low, own_down, send_down, down),
                (c - d, c - d, c - d >= 0, c < col_count - 1, before_high, own_up, send_up, up),
            ):

                @pl.when((unit == 0) & exists)
                def _():
                    ref = own_block(z)
                    arrived(ref, recv_z.at[z, 0])

                    @pl.when(onward)
                    def _():
                        remote(ref, ref, own_sems.at[z], recv_z.at[z, 0], target).start()

                @pl.when((unit >= 1) & exists & ((unit < chunks) | (onward & (unit == chunks))))
                def _():
                    arrived(chunk(z, unit - 1), recv_z.at[z, unit])

                    @pl.when(onward)
                    def _():
                        forward(z, unit, sems, target, last_hop, k)

                @pl.when((unit == chunks) & exists & jnp.logical_not(onward))
                def _():
                    arrived(early(z), recv_z.at[z, unit])

        @pl.when(t == FACTS_STEP)
        def _():
            arrived(other_facts, facts_sem.at[1])
            for p in range(1, row_count):
                ref = facts.at[:, r]
                remote(ref, ref, facts_sem.at[2], facts_sem.at[3], (peers[p], c)).start()

        @pl.when((t == slab_step) & (r == 0))
        def _():
            own_copy.wait()
            source = held.at[:, :, pl.ds(pl.multiple_of(c * columns, columns), columns)]
            for p in range(1, row_count):
                remote(source, slab, slab_sem.at[0], slab_sem.at[1], (p, c)).start()
            local_slab = pltpu.make_async_copy(source, slab, slab_sem.at[2])
            local_slab.start()
            local_slab.wait()

        @pl.when(t == solve_step)
        def _():
            @pl.when(r > 0)
            def _():
                own_copy.wait()
                arrived(slab, slab_sem.at[1])

            arrived(rest, facts_sem.at[3])
            for z in range(col_count):
                for k in range(row_count):
                    spread_facts[pl.ds((z * row_count + k) * rows_dev, rows_dev), :] = jnp.broadcast_to(
                        facts[z, k], (rows_dev, LANES)
                    )
            out = eliminate(
                spread_facts[...],
                slab[...].reshape(col_count * block, columns).astype(jnp.float32),
                order,
                arcs,
                rows_dev,
            ).reshape(col_count, block, columns)
            for edge, first in ((0, 1), (col_count - 1, 0)):

                @pl.when(c == edge)
                def _():
                    piece[...] = jnp.zeros_like(piece)
                    for z in range(first, first + col_count - 1):
                        held[z, rows_dev:block, rows - narrow : rows] = jnp.zeros(
                            (block - rows_dev, narrow), jnp.bfloat16
                        )

            for k in range(row_count):
                at = pl.ds(pl.multiple_of(peers[k] * rows_dev, rows_dev), rows_dev)
                elim[:, at, :] = out[:, k * rows_dev : (k + 1) * rows_dev, :]

        @pl.when(t == chunks + 1)
        def _():
            sent = design.at[:, pl.ds(0, (row_count - 1) * rows)]
            arrived(sent, send_in.at[0])
            arrived(other_facts, facts_sem.at[0])
            arrived(rest, facts_sem.at[2])

            @pl.when(r == 0)
            def _():
                share = held.at[:, :, pl.ds(0, (row_count - 1) * columns)]
                arrived(share, slab_sem.at[0])

        here = lax.min(lax.max(t - (col_count - 1) * SKEW, 0), chunks - LEFT)
        before = lax.min(lax.max(t - 1 - (col_count - 1) * SKEW, 0), chunks - LEFT)

        @pl.when(t >= solve_step)
        def _():
            def form(j, _):
                ready[part(j), :] = product_tile(held, elim, j * width, width)
                return 0

            lax.fori_loop(lax.select(t == solve_step, 0, before), here, form, 0)

        return 0

    slab_step = slab_chunks + (col_count - 1) * SKEW
    solve_step = slab_step + SOLVE_AFTER
    lax.fori_loop(0, chunks + 1 + (col_count - 1) * SKEW, step, 0)

    for z in range(col_count):
        for sends, last_hop, own_sems, sems in (
            ((c > 0) & (z >= c), before_low, own_down, send_down),
            ((c < col_count - 1) & (z <= c), before_high, own_up, send_up),
        ):

            @pl.when(sends)
            def _():
                arrived(own_block(z), own_sems.at[z])

            @pl.when(sends & last_hop)
            def _():
                arrived(held.at[z, others, pl.ds(0, rows - narrow)], sems.at[z])

            @pl.when(sends & jnp.logical_not(last_hop))
            def _():
                arrived(held.at[z, others, :], sems.at[z])

    @pl.when(before_low | before_high)
    def _():
        arrived(piece, own_sem.at[3])


def in_hbm(array):
    return pltpu.with_memory_space_constraint(array, pltpu.HBM)


def gather(design, arc_partials, arc_id, arc_weight, row_count, col_count):
    rows_dev, coefficients = design.shape
    rows = coefficients // row_count
    columns = SLAB // col_count
    block = rows_dev * row_count
    width = chunk_width(rows)
    chunks = rows // width
    dma = pltpu.SemaphoreType.DMA
    partials = arc_partials.transpose(1, 0, 2)
    in_vmem = pl.BlockSpec(memory_space=pltpu.VMEM)
    return pl.pallas_call(
        functools.partial(gather_kernel, row_count, col_count, width),
        out_shape=(
            pltpu.VMEM((col_count, block, rows), jnp.bfloat16),
            pltpu.VMEM((col_count, block, columns), jnp.bfloat16),
            pltpu.VMEM((rows - LEFT * width, columns), jnp.float32),
            pltpu.VMEM((col_count - 1, block - rows_dev, narrow_width(width, col_count)), jnp.bfloat16),
        ),
        in_specs=[
            pl.BlockSpec(memory_space=pltpu.HBM),
            pl.BlockSpec(memory_space=pltpu.HBM),
            pl.BlockSpec(memory_space=pltpu.SMEM),
            pl.BlockSpec(memory_space=pltpu.HBM),
        ],
        out_specs=(in_vmem,) * 4,
        scratch_shapes=[
            pltpu.VMEM((col_count, block, columns), jnp.bfloat16),
            pltpu.VMEM((col_count, row_count, 1, LANES), jnp.float32),
            pltpu.VMEM((col_count * block, LANES), jnp.float32),
            pltpu.VMEM(partials.shape, jnp.float32),
            pltpu.SMEM(arc_weight.shape, jnp.float32),
            dma((col_count, chunks + 1)),
            dma((col_count,)),
            dma((col_count,)),
            dma((col_count,)),
            dma((col_count,)),
            dma((chunks,)),
            dma((1,)),
            dma((4,)),
            dma((3,)),
            dma((4,)),
        ],
        compiler_params=pltpu.CompilerParams(
            collective_id=0, has_side_effects=True, vmem_limit_bytes=16 << 20
        ),
        name="gather",
    )(in_hbm(design), in_hbm(partials), arc_id, in_hbm(arc_weight))


def finish_kernel(size, held, elim, ready, out, partial, tile, sems):
    rows = out.shape[0]
    count = ready.shape[0] // size
    narrow = partial.shape[0]
    copies = [
        pltpu.make_async_copy(ready.at[at, :], out.at[at, :], sems.at[i])
        for i, at in enumerate(pl.ds(i * size, size) for i in range(count))
    ]
    for copy in copies:
        copy.start()
    for k, (start, length) in enumerate(((rows - LEFT * size, size), (rows - size, size - narrow))):
        tile[k, 0:length, :] = product_tile(held, elim, start, length)
        to = out.at[pl.ds(start, length), :]
        copies.append(pltpu.make_async_copy(tile.at[k, pl.ds(0, length), :], to, sems.at[count + k]))
        copies[-1].start()
    partial[...] = product_tile(held, elim, rows - narrow, narrow)
    for copy in copies:
        copy.wait()


def finish(held, elim, ready):
    col_count, block, rows = held.shape
    columns = elim.shape[2]
    width = chunk_width(rows)
    in_vmem = pl.BlockSpec(memory_space=pltpu.VMEM)
    return pl.pallas_call(
        functools.partial(finish_kernel, width),
        out_shape=(
            jax.ShapeDtypeStruct((rows, columns), jnp.float32),
            pltpu.VMEM((narrow_width(width, col_count), columns), jnp.float32),
        ),
        in_specs=[in_vmem, in_vmem, in_vmem],
        out_specs=(pl.BlockSpec(memory_space=pl.ANY), in_vmem),
        scratch_shapes=[
            pltpu.VMEM((LEFT, width, columns), jnp.float32),
            pltpu.SemaphoreType.DMA((rows // width,)),
        ],
        compiler_params=pltpu.CompilerParams(vmem_limit_bytes=12 << 20),
        cost_estimate=pl.CostEstimate(
            flops=2 * LEFT * col_count * block * width * columns,
            bytes_accessed=4 * rows * columns,
            transcendentals=0,
        ),
        name="finish",
    )(held, elim, ready)


def last_kernel(scale, rows_dev, elim, partial, arrived, total, out, tile, sem):
    col_count, block, _ = elim.shape
    narrow = partial.shape[0]
    first = lax.select(lax.axis_index("col") == 0, 1, 0)
    late = elim[pl.ds(first, col_count - 1), rows_dev:block, :].reshape(-1, tile.shape[1])
    rows = arrived[...].reshape(late.shape[0], narrow)
    tile[...] = partial[...] + scale * lax.dot_general(
        rows, late, (((0,), (0,)), ((), ())), preferred_element_type=jnp.float32
    )
    copy = pltpu.make_async_copy(tile, out.at[pl.ds(out.shape[0] - narrow, narrow), :], sem)
    copy.start()
    copy.wait()


def last(elim, partial, arrived, total, rows_dev):
    col_count, block, columns = elim.shape
    in_vmem = pl.BlockSpec(memory_space=pltpu.VMEM)
    in_place = pl.BlockSpec(memory_space=pl.ANY)
    return pl.pallas_call(
        functools.partial(last_kernel, 1.0 / (col_count * block), rows_dev),
        out_shape=jax.ShapeDtypeStruct(total.shape, jnp.float32),
        in_specs=[in_vmem, in_vmem, in_vmem, in_place],
        out_specs=in_place,
        input_output_aliases={3: 0},
        scratch_shapes=[
            pltpu.VMEM(partial.shape, jnp.float32),
            pltpu.SemaphoreType.DMA,
        ],
        compiler_params=pltpu.CompilerParams(vmem_limit_bytes=12 << 20),
        name="last",
    )(elim, partial, arrived, total)


def local(design, arc_partials, arc_id, arc_weight):
    row_count, col_count = lax.axis_size("row"), lax.axis_size("col")
    held, elim, ready, piece = gather(design, arc_partials, arc_id, arc_weight, row_count, col_count)
    pairs = [(1, 0), (0, 1), (col_count - 2, col_count - 1), (col_count - 1, col_count - 2)]
    arrived = lax.ppermute(piece, "col", pairs)
    total, partial = finish(held, elim, ready)
    return last(elim, partial, arrived, total, design.shape[0])


def solution(mesh):
    placed = (P(("row", "col"), None), P(("row", "col"), None, None), P(("row", "col")), P())
    return jax.shard_map(
        local, mesh=mesh, in_specs=placed, out_specs=P("row", "col"), check_vma=False
    )
```
